512 devices in a mesh: frame: 64 (over x, y_hi, z), group: 8 (over y_lo, core).
Axes of the slice: x: 4, y: 8 (y_hi: 2, y_lo: 4; y = y_hi * 4 + y_lo), z: 8, core: 2. Of those that a mesh axis runs over, the one named last changes fastest.
Arguments:
- queries: bfloat16 [8192, 8192], P('frame', 'group'), may hold values from -6 to 6
- keys: bfloat16 [8192, 1024], P('frame', 'group'), may hold values from -50 to 50
- values: bfloat16 [8192, 1024], P('frame', 'group'), may hold values from -6 to 6
- q_gain: float32 [128], replicated, may hold values from 0.4 to 2.5
- frame_bounds: int32 [2, 8192], P(None, 'frame'), may hold values from 0 to 64, as said below
- output_weight: bfloat16 [8, 1024, 4096], P('group', 'frame'), may hold values from -0.25 to 0.25
- attn_gate: float32 [1], replicated, may hold values from 0.4 to 1.6
Outputs:
- projected: bfloat16 [8192, 4096], P('frame', 'group')
The draws below stay inside these ranges and needn't reach their ends.
Inputs may be any that keep to these rules, and one draw needn't show every extreme that they name: `frame_bounds`: row 0 is below row 1 for every text token.
All inputs are finite; a program needn't handle non-finite values.
Results may differ from the reference program's by a relative error of at most 0.008.
The reference program's roundings to bfloat16 on the way count: a program that leaves them out, or rounds other values in their place, can miss the bound.
Values may be sent and summed in bfloat16 or wider, within the bound.
No kernel may reach another device: no remote copies, remote signals or barrier semaphores. Data moves between devices by JAX's collectives and lax.ppermute only.
A program may use at most 64 MiB of HBM per device.

```python
import math
import jax
import jax.numpy as jnp
from jax import lax

HEAD_WIDTH = 128
QUERY_PER_GROUP = 8
OUTPUT_FEATURES = 4096
V_DEV = 128
KEY_VALUE_HEADS = 8
QUERY_HEADS = 64
TEXT_TOKENS = 8192
VISUAL_TOKENS = 8192
NBLK = 64


def frame_limits(key):
    lower_block = jax.random.randint(jax.random.fold_in(key, 31), (TEXT_TOKENS,), 0, NBLK)
    span_count = jax.random.randint(jax.random.fold_in(key, 32), (TEXT_TOKENS,), 1, NBLK + 1)
    upper_block = jnp.minimum(lower_block + span_count, NBLK)
    lower_block = lower_block.at[0].set(0)
    upper_block = upper_block.at[0].set(NBLK)
    return (lower_block.astype(jnp.int32), upper_block.astype(jnp.int32))


def draw_frame_bounds(key, part):
    lower_block, upper_block = frame_limits(key)
    return jnp.stack([lower_block, upper_block]).astype(jnp.int32)


def row_scales(key):
    return jnp.exp(jax.random.uniform(jax.random.fold_in(key, 42), (VISUAL_TOKENS, 1), jnp.float32, math.log(2.5), math.log(3.0)))


def draw_keys(key, part):
    sampled_values = jnp.clip(jax.random.normal(jax.random.fold_in(key, 41), (VISUAL_TOKENS, KEY_VALUE_HEADS * HEAD_WIDTH), jnp.float32), -6.0, 6.0)
    result = sampled_values * row_scales(key)
    return result.astype(jnp.bfloat16)


def draw_queries(key, part):
    sampled_values = jnp.clip(jax.random.normal(jax.random.fold_in(key, 51), (TEXT_TOKENS, QUERY_HEADS * HEAD_WIDTH), jnp.float32), -6.0, 6.0)
    return sampled_values.astype(jnp.bfloat16)


def shard_levels(own_key, extent, cuts, smallest, high):
    def one(axis_at, shards_of):
        heights = jax.random.uniform(jax.random.fold_in(jax.random.fold_in(own_key, 6), axis_at), (shards_of,), jnp.float32, smallest / len(cuts), high / len(cuts))
        return jnp.repeat(jnp.exp(heights), extent[axis_at] // shards_of).reshape((-1,) + (1,) * (len(extent) - axis_at - 1))

    gain = one(*cuts[0])
    for cut in cuts[1:]:
        gain = gain * one(*cut)
    return gain


def normal_values(rng, extent, scale, bound, pieces=(), dtype=jnp.bfloat16):
    drawn = jax.random.normal(rng, extent, jnp.float32) * scale
    if len(pieces) > 0:
        drawn = shard_levels(rng, extent, pieces, -0.22, 0.18) * drawn
    return jnp.clip(drawn, min=-bound, max=bound).astype(dtype)


def setup_inputs(seed: int = 0) -> dict:
    streams_of = jax.random.split(jax.random.key(seed), 8)
    queries = draw_queries(jax.random.fold_in(streams_of[7], 71), 0)
    keys = draw_keys(jax.random.fold_in(streams_of[7], 71), 0)
    values = normal_values(streams_of[2], (VISUAL_TOKENS, KEY_VALUE_HEADS * HEAD_WIDTH), 1.0, 6.0, ((0, 64), (1, 8)))
    q_gain = jnp.clip(jnp.exp(jax.random.uniform(streams_of[3], (HEAD_WIDTH,), jnp.float32, math.log(0.4), math.log(2.5))), 0.4, 2.5)
    frame_bounds = draw_frame_bounds(jax.random.fold_in(streams_of[7], 71), 0)
    output_weight = normal_values(streams_of[5], (KEY_VALUE_HEADS, QUERY_PER_GROUP * HEAD_WIDTH, OUTPUT_FEATURES), 512 ** -0.5, 0.25, ((0, 8), (1, 64)))
    attn_gate = jnp.clip(jax.random.uniform(streams_of[6], (1,), jnp.float32, 0.4, 1.6), 0.4, 1.6)
    return dict(queries=queries, keys=keys, values=values, q_gain=q_gain, frame_bounds=frame_bounds, output_weight=output_weight, attn_gate=attn_gate)


def reference(queries, keys, values, q_gain, frame_bounds, output_weight, attn_gate):
    as_float = queries.astype(jnp.float32).reshape(TEXT_TOKENS, QUERY_HEADS, HEAD_WIDTH)
    normalized_input = as_float * lax.rsqrt(lax.optimization_barrier(jnp.mean(as_float * as_float, axis=-1, keepdims=True)) + 1e-05) * q_gain
    normalized_input = normalized_input.astype(jnp.bfloat16).reshape(TEXT_TOKENS, KEY_VALUE_HEADS, QUERY_PER_GROUP * HEAD_WIDTH)
    text_block = math.gcd(TEXT_TOKENS, 512)
    block_count = TEXT_TOKENS // text_block
    lower_rows = frame_bounds[0].reshape(block_count, text_block)
    upper_rows = frame_bounds[1].reshape(block_count, text_block)
    score_scale = 1.0 / math.sqrt(HEAD_WIDTH)
    block_ids = (jnp.arange(VISUAL_TOKENS) // V_DEV).astype(jnp.int32)

    def single_head(head_index):
        head_keys = lax.dynamic_slice_in_dim(keys, head_index * HEAD_WIDTH, HEAD_WIDTH, 1)
        head_values = lax.dynamic_slice_in_dim(values, head_index * HEAD_WIDTH, HEAD_WIDTH, 1)
        head_queries = lax.dynamic_index_in_dim(normalized_input, head_index, 1, keepdims=False)
        head_queries = head_queries.reshape(block_count, text_block * QUERY_PER_GROUP, HEAD_WIDTH)

        def one_block(packed):
            query_rows, lower_bound, upper_bound = packed
            scores = jnp.dot(query_rows, head_keys.T, preferred_element_type=jnp.float32) * score_scale
            lower_here = jnp.repeat(lower_bound, QUERY_PER_GROUP)[:, None]
            upper_here = jnp.repeat(upper_bound, QUERY_PER_GROUP)[:, None]
            allowed = (block_ids[None, :] >= lower_here) & (block_ids[None, :] < upper_here)
            masked = jnp.where(allowed, scores, -1e+30)
            row_max = lax.optimization_barrier(jnp.max(masked, axis=1, keepdims=True))
            exp_weights = jnp.where(allowed, jnp.exp(masked - row_max), 0.0)
            denominator = lax.optimization_barrier(jnp.sum(exp_weights, axis=1, keepdims=True))
            numerator = jnp.dot(exp_weights.astype(jnp.bfloat16), head_values, preferred_element_type=jnp.float32)
            return (numerator / denominator).astype(jnp.bfloat16).reshape(text_block, QUERY_PER_GROUP * HEAD_WIDTH)
        return lax.map(one_block, (head_queries, lower_rows, upper_rows)).reshape(TEXT_TOKENS, QUERY_PER_GROUP * HEAD_WIDTH)
    per_head_output = lax.map(single_head, jnp.arange(KEY_VALUE_HEADS).astype(jnp.int32))
    attended = jnp.transpose(per_head_output, (1, 0, 2)).reshape(TEXT_TOKENS, QUERY_HEADS * HEAD_WIDTH)
    summed = jnp.dot(attended, output_weight.reshape(QUERY_HEADS * HEAD_WIDTH, OUTPUT_FEATURES), preferred_element_type=jnp.float32)
    return (jnp.tanh(attn_gate[0]) * summed).astype(jnp.bfloat16)
```

```python
import math

import jax
import jax.numpy as jnp
from jax import lax
from jax.experimental import pallas as pl
from jax.experimental.pallas import tpu as pltpu
from jax.sharding import Mesh, PartitionSpec as P


D = 128
HEADS = 8
TOK = 128
ROWS = HEADS * TOK
SUB = 8
KEYS = 4
WIDE = 256
LOW = -1e30
EXP2_SCALE = math.log2(math.e) / math.sqrt(D)


def shift(value, axis, steps):
    count = lax.axis_size(axis)
    return lax.ppermute(value, axis, [(s, (s + steps) % count) for s in range(count)])


def attention_kernel(n_chunks, first, last, ids_ref, *refs):
    refs = list(refs)
    bounds_ref = refs.pop(0)
    chunks = [refs.pop(0) for _ in range(n_chunks)]
    if first:
        q_ref, gain_ref = refs.pop(0), refs.pop(0)
    else:
        nq_in, m_in, l_in, acc_in = [refs.pop(0) for _ in range(4)]
    if last:
        out_ref = refs.pop(0)
    else:
        nq_out, m_out, l_out, acc_out = [refs.pop(0) for _ in range(4)]
    if first:
        nq_ref = nq_out
        for h in range(HEADS):
            x = q_ref[:, h * D : (h + 1) * D].astype(jnp.float32)
            mean = jnp.mean(x * x, axis=-1, keepdims=True)
            x = x * lax.rsqrt(mean + 1e-05) * gain_ref[...]
            nq_ref[h * TOK : (h + 1) * TOK, :] = x.astype(jnp.bfloat16)
    else:
        nq_ref = nq_in
    lower = jnp.concatenate([bounds_ref[0:1, :]] * (WIDE // TOK), axis=1)
    upper = jnp.concatenate([bounds_ref[1:2, :]] * (WIDE // TOK), axis=1)
    for w in range(ROWS // WIDE):
        cols = slice(w * WIDE, (w + 1) * WIDE)
        q = nq_ref[cols, :]
        if first:
            state = (
                jnp.full((1, WIDE), LOW, jnp.float32),
                jnp.zeros((8, WIDE), jnp.float32),
                jnp.zeros((D, WIDE), jnp.float32),
            )
        else:
            state = (m_in[:, cols], l_in[:, cols], acc_in[:, cols])
        for c, chunk in enumerate(chunks):

            def step(i, state, c=c, chunk=chunk, q=q):
                m, l, acc = state
                at = pl.ds(i * KEYS, KEYS)
                k = chunk[at, 0].reshape(KEYS * D, D)
                v = chunk[at, 1].reshape(KEYS * D, D)
                s = lax.dot_general(
                    k, q, (((1,), (1,)), ((), ())), preferred_element_type=jnp.float32
                )
                allowed = []
                new = m
                for j in range(KEYS):
                    block = ids_ref[c * SUB + i * KEYS + j]
                    ok = (lower <= block) & (block < upper)
                    top = jnp.max(s[j * D : (j + 1) * D], axis=0, keepdims=True)
                    new = jnp.maximum(new, jnp.where(ok, top, LOW))
                    allowed.append(ok)
                factor = jnp.exp2((m - new) * EXP2_SCALE)
                l = l * factor
                parts = []
                for j in range(KEYS):
                    base = jnp.where(allowed[j], new * EXP2_SCALE, -LOW)
                    p = jnp.exp2(s[j * D : (j + 1) * D] * EXP2_SCALE - base)
                    l = l + jnp.sum(p.reshape(D // 8, 8, WIDE), axis=0)
                    parts.append(p.astype(jnp.bfloat16))
                p = jnp.concatenate(parts, axis=0)
                acc = acc * factor + lax.dot_general(
                    v, p, (((0,), (0,)), ((), ())), preferred_element_type=jnp.float32
                )
                return new, l, acc

            state = lax.fori_loop(0, SUB // KEYS, step, state)
        m, l, acc = state
        if last:
            o = acc / jnp.sum(l, axis=0, keepdims=True)
            for u in range(WIDE // TOK):
                head = w * (WIDE // TOK) + u
                out_ref[:, head * D : (head + 1) * D] = (
                    o[:, u * TOK : (u + 1) * TOK].T.astype(jnp.bfloat16)
                )
        else:
            m_out[:, cols] = m
            l_out[:, cols] = l
            acc_out[:, cols] = acc
    if not first and not last:
        nq_out[...] = nq_in[...]


def attend(ids, bounds, chunks, start, state, last):
    first = state is None
    vm = pl.BlockSpec(memory_space=pltpu.VMEM)
    carried = (
        jax.ShapeDtypeStruct((ROWS, D), jnp.bfloat16),
        jax.ShapeDtypeStruct((1, ROWS), jnp.float32),
        jax.ShapeDtypeStruct((8, ROWS), jnp.float32),
        jax.ShapeDtypeStruct((D, ROWS), jnp.float32),
    )
    out_shape = jax.ShapeDtypeStruct((TOK, ROWS), jnp.bfloat16) if last else carried
    extra = start if first else state
    n_keys = len(chunks) * SUB * D

    def body(*refs):
        attention_kernel(len(chunks), first, last, *refs)

    return pl.pallas_call(
        body,
        out_shape=out_shape,
        in_specs=[pl.BlockSpec(memory_space=pltpu.SMEM)]
        + [vm] * (1 + len(chunks) + len(extra)),
        out_specs=vm if last else (vm,) * 4,
        cost_estimate=pl.CostEstimate(
            flops=4 * ROWS * n_keys * D,
            bytes_accessed=n_keys * D * 4 + ROWS * D * 12,
            transcendentals=ROWS * n_keys,
        ),
        compiler_params=pltpu.CompilerParams(vmem_limit_bytes=40 << 20),
    )(ids, bounds, *chunks, *extra)


def project_kernel(a_ref, w_ref, out_ref):
    total = None
    for x in range(4):
        w = w_ref[:, x].reshape(256, 512)
        part = jnp.dot(
            a_ref[:, x * 256 : (x + 1) * 256], w, preferred_element_type=jnp.float32
        )
        total = part if total is None else total + part
    out_ref[...] = total.reshape(4, 1, TOK, 512)


def project(attended, weight):
    return pl.pallas_call(
        project_kernel,
        grid=(2,),
        out_shape=jax.ShapeDtypeStruct((4, 2, TOK, 512), jnp.float32),
        in_specs=[
            pl.BlockSpec((4 * TOK, ROWS), lambda i: (0, 0)),
            pl.BlockSpec((16, 4, 16, 512), lambda i: (0, 0, 0, i)),
        ],
        out_specs=pl.BlockSpec((4, 1, TOK, 512), lambda i: (0, i, 0, 0)),
        cost_estimate=pl.CostEstimate(
            flops=2 * 512 * 1024 * 1024, bytes_accessed=5 << 20, transcendentals=0
        ),
        compiler_params=pltpu.CompilerParams(vmem_limit_bytes=32 << 20),
    )(attended, weight)


def local(queries, keys, values, q_gain, frame_bounds, output_weight, attn_gate):
    ax, ay, az = lax.axis_index("x"), lax.axis_index("yh"), lax.axis_index("z")
    quarters = output_weight[0].reshape(16, 4, 1024).transpose(1, 0, 2).reshape(64, 1024)
    quarter = lax.all_to_all(quarters, "x", split_axis=0, concat_axis=0, tiled=True)
    weight = lax.all_gather(quarter, ("yh", "z"), axis=0, tiled=True)
    weight = weight.reshape(16, 4, 16, 1024)

    own = jnp.stack([keys, values])[None]
    pair = jnp.concatenate([own, shift(own, "yh", 1)])
    chunk = jnp.concatenate(
        [pair, shift(pair, "x", 1), shift(pair, "x", -1), shift(pair, "x", 2)]
    )
    hops = ([0, -1, 1, 2], [0, -1, 1, -2, 2, -3, 3, -4])
    in_chunk = jnp.stack(
        [((ax + h) % 4) * 16 + ((ay + y) % 2) * 8 for h in hops[0] for y in (0, 1)]
    ).astype(jnp.int32)
    ids = [in_chunk + (az + h) % 8 for h in hops[1]]

    right, left = [chunk], [chunk]
    for s in range(4):
        right.append(shift(right[-1], "z", 1))
        if s < 3:
            left.append(shift(left[-1], "z", -1))
    start = (queries, q_gain[None, :])
    state = attend(ids[0], frame_bounds, [chunk], start, None, False)
    for s in range(1, 4):
        state = attend(
            jnp.concatenate(ids[2 * s - 1 : 2 * s + 1]),
            frame_bounds,
            [right[s], left[s]],
            start,
            state,
            False,
        )
    attended = attend(ids[7], frame_bounds, [right[4]], start, state, True)

    rel = [0, -1, 1, 2]
    gathered = jnp.concatenate(
        [attended] + [shift(attended, "x", -r) for r in rel[1:]], axis=0
    )
    partial = project(gathered, weight).reshape(1024, 512)
    combined = lax.psum_scatter(partial, ("yl", "c"), scatter_dimension=0, tiled=True)
    result = (jnp.tanh(attn_gate[0]) * combined).astype(jnp.bfloat16)
    pairs = [
        (x * 4 + y, ((x + rel[y]) % 4) * 4 + x) for x in range(4) for y in range(4)
    ]
    return lax.ppermute(result, ("x", "yl"), pairs)


def solution(mesh):
    fine = Mesh(mesh.devices.reshape(4, 2, 8, 4, 2), ("x", "yh", "z", "yl", "c"))
    frame, group = ("x", "yh", "z"), ("yl", "c")
    placed = (
        P(frame, group),
        P(frame, group),
        P(frame, group),
        P(),
        P(None, frame),
        P(group, frame, None),
        P(),
    )
    return jax.shard_map(
        local, mesh=fine, in_specs=placed, out_specs=P(frame, group), check_vma=False
    )
```

```python
import math

import jax
import jax.numpy as jnp
from jax import lax
from jax.experimental import pallas as pl
from jax.experimental.pallas import tpu as pltpu
from jax.sharding import Mesh, PartitionSpec as P


D = 128
HEADS = 8
TOK = 128
ROWS = HEADS * TOK
SUB = 8
KEYS = 4
WIDE = 256
LOW = -1e30
EXP2_SCALE = math.log2(math.e) / math.sqrt(D)


def shift(value, axis, steps):
    count = lax.axis_size(axis)
    return lax.ppermute(value, axis, [(s, (s + steps) % count) for s in range(count)])


def attention_kernel(n_chunks, first, last, ids_ref, *refs):
    refs = list(refs)
    bounds_ref = refs.pop(0)
    chunks = [refs.pop(0) for _ in range(n_chunks)]
    if first:
        q_ref, gain_ref = refs.pop(0), refs.pop(0)
    else:
        nq_in, m_in, l_in, acc_in = [refs.pop(0) for _ in range(4)]
    if last:
        out_ref = refs.pop(0)
    else:
        nq_out, m_out, l_out, acc_out = [refs.pop(0) for _ in range(4)]
    if first:
        nq_ref = nq_out
        for h in range(HEADS):
            x = q_ref[:, h * D : (h + 1) * D].astype(jnp.float32)
            mean = jnp.mean(x * x, axis=-1, keepdims=True)
            x = x * lax.rsqrt(mean + 1e-05) * gain_ref[...]
            nq_ref[h * TOK : (h + 1) * TOK, :] = x.astype(jnp.bfloat16)
    else:
        nq_ref = nq_in
    lower = jnp.concatenate([bounds_ref[0:1, :]] * (WIDE // TOK), axis=1)
    upper = jnp.concatenate([bounds_ref[1:2, :]] * (WIDE // TOK), axis=1)
    cols = [slice(w * WIDE, (w + 1) * WIDE) for w in range(ROWS // WIDE)]
    if first:
        state = [
            (
                jnp.full((1, WIDE), LOW, jnp.float32),
                jnp.zeros((8, WIDE), jnp.float32),
                jnp.zeros((D, WIDE), jnp.float32),
            )
            for _ in cols
        ]
    else:
        state = [(m_in[:, c], l_in[:, c], acc_in[:, c]) for c in cols]
    units = [
        (c, i, w)
        for c in range(n_chunks)
        for i in range(SUB // KEYS)
        for w in range(len(cols))
    ]

    def score(unit):
        c, i, w = unit
        k = chunks[c][i * KEYS : (i + 1) * KEYS, 0].reshape(KEYS * D, D)
        return lax.dot_general(
            k,
            nq_ref[cols[w], :],
            (((1,), (1,)), ((), ())),
            preferred_element_type=jnp.float32,
        )

    def soften(unit, s, m, l):
        c, i, _ = unit
        allowed = []
        new = m
        for j in range(KEYS):
            block = ids_ref[c * SUB + i * KEYS + j]
            ok = (lower <= block) & (block < upper)
            top = jnp.max(s[j * D : (j + 1) * D], axis=0, keepdims=True)
            new = jnp.maximum(new, jnp.where(ok, top, LOW))
            allowed.append(ok)
        factor = jnp.exp2((m - new) * EXP2_SCALE)
        l = l * factor
        parts = []
        for j in range(KEYS):
            base = jnp.where(allowed[j], new * EXP2_SCALE, -LOW)
            p = jnp.exp2(s[j * D : (j + 1) * D] * EXP2_SCALE - base)
            l = l + jnp.sum(p.reshape(D // 8, 8, WIDE), axis=0)
            parts.append(p.astype(jnp.bfloat16))
        return jnp.concatenate(parts, axis=0), new, l, factor

    def gather(unit, p, acc, factor):
        c, i, _ = unit
        v = chunks[c][i * KEYS : (i + 1) * KEYS, 1].reshape(KEYS * D, D)
        return acc * factor + lax.dot_general(
            v, p, (((0,), (0,)), ((), ())), preferred_element_type=jnp.float32
        )

    ahead = score(units[0])
    pending = None
    for at, unit in enumerate(units):
        s = ahead
        if at + 1 < len(units):
            ahead = score(units[at + 1])
        w = unit[2]
        m, l, acc = state[w]
        p, m, l, factor = soften(unit, s, m, l)
        if pending is not None:
            u, p0, f0 = pending
            m0, l0, acc0 = state[u[2]]
            state[u[2]] = (m0, l0, gather(u, p0, acc0, f0))
        state[w] = (m, l, state[w][2])
        pending = (unit, p, factor)
    u, p0, f0 = pending
    m0, l0, acc0 = state[u[2]]
    state[u[2]] = (m0, l0, gather(u, p0, acc0, f0))

    for w, (m, l, acc) in enumerate(state):
        if last:
            o = acc / jnp.sum(l, axis=0, keepdims=True)
            for u in range(WIDE // TOK):
                head = w * (WIDE // TOK) + u
                out_ref[:, head * D : (head + 1) * D] = (
                    o[:, u * TOK : (u + 1) * TOK].T.astype(jnp.bfloat16)
                )
        else:
            m_out[:, cols[w]] = m
            l_out[:, cols[w]] = l
            acc_out[:, cols[w]] = acc
    if not first and not last:
        nq_out[...] = nq_in[...]


def attend(ids, bounds, chunks, start, state, last):
    first = state is None
    vm = pl.BlockSpec(memory_space=pltpu.VMEM)
    carried = (
        jax.ShapeDtypeStruct((ROWS, D), jnp.bfloat16),
        jax.ShapeDtypeStruct((1, ROWS), jnp.float32),
        jax.ShapeDtypeStruct((8, ROWS), jnp.float32),
        jax.ShapeDtypeStruct((D, ROWS), jnp.float32),
    )
    out_shape = jax.ShapeDtypeStruct((TOK, ROWS), jnp.bfloat16) if last else carried
    extra = start if first else state
    n_keys = len(chunks) * SUB * D

    def body(*refs):
        attention_kernel(len(chunks), first, last, *refs)

    return pl.pallas_call(
        body,
        out_shape=out_shape,
        in_specs=[pl.BlockSpec(memory_space=pltpu.SMEM)]
        + [vm] * (1 + len(chunks) + len(extra)),
        out_specs=vm if last else (vm,) * 4,
        cost_estimate=pl.CostEstimate(
            flops=4 * ROWS * n_keys * D,
            bytes_accessed=n_keys * D * 4 + ROWS * D * 12,
            transcendentals=ROWS * n_keys,
        ),
        compiler_params=pltpu.CompilerParams(vmem_limit_bytes=40 << 20),
    )(ids, bounds, *chunks, *extra)


def project_kernel(col_ref, a_ref, w_ref, out_ref):
    total = None
    for x in range(4):
        w = jnp.concatenate([w_ref[:, 0, x], w_ref[:, 1, x]]).reshape(256, 512)
        part = jnp.dot(
            a_ref[:, x * 256 : (x + 1) * 256], w, preferred_element_type=jnp.float32
        )
        total = part if total is None else total + part
    out_ref[...] = total.reshape(4, TOK, 512)


def project(column, attended, weight):
    return pl.pallas_call(
        project_kernel,
        grid_spec=pltpu.PrefetchScalarGridSpec(
            num_scalar_prefetch=1,
            grid=(1,),
            in_specs=[
                pl.BlockSpec((4 * TOK, ROWS), lambda i, col: (0, 0)),
                pl.BlockSpec((8, 2, 4, 16, 512), lambda i, col: (0, 0, 0, 0, col[0])),
            ],
            out_specs=pl.BlockSpec((4, TOK, 512), lambda i, col: (0, 0, 0)),
        ),
        out_shape=jax.ShapeDtypeStruct((4, TOK, 512), jnp.float32),
        cost_estimate=pl.CostEstimate(
            flops=512 * 1024 * 1024, bytes_accessed=3 << 20, transcendentals=0
        ),
        compiler_params=pltpu.CompilerParams(vmem_limit_bytes=32 << 20),
    )(column, attended, weight)


def work(queries, keys, values, q_gain, frame_bounds, output_weight, attn_gate):
    ax, ay, az = lax.axis_index("x"), lax.axis_index("yh"), lax.axis_index("z")
    core = lax.axis_index("c")

    own = jnp.stack([keys, values])[None]
    other = shift(own, "yh", 1)
    quarter = output_weight[0].reshape(16, 4, 1024).transpose(1, 0, 2)
    quarter = lax.all_to_all(
        quarter.reshape(64, 1024), "x", split_axis=0, concat_axis=0, tiled=True
    )
    partner = shift(quarter, "yh", 1)
    both = jnp.stack(
        [jnp.where(ay == 0, quarter, partner), jnp.where(ay == 0, partner, quarter)]
    )
    weight = lax.all_gather(both.reshape(128, 1024), "z", axis=0, tiled=True)
    weight = weight.reshape(8, 2, 4, 16, 1024)

    pair = jnp.concatenate([own, other])
    chunk = jnp.concatenate(
        [pair, shift(pair, "x", 1), shift(pair, "x", -1), shift(pair, "x", 2)]
    )
    hops = ([0, -1, 1, 2], [0, -1, 1, -2, 2, -3, 3, -4])
    in_chunk = jnp.stack(
        [((ax + h) % 4) * 16 + ((ay + y) % 2) * 8 for h in hops[0] for y in (0, 1)]
    ).astype(jnp.int32)
    ids = [in_chunk + (az + h) % 8 for h in hops[1]]

    right, left = [chunk], [chunk]
    for s in range(1, 5):
        right.append(shift(right[-1], "z", 1))
        if s < 4:
            left.append(shift(left[-1], "z", -1))
    start = (queries, q_gain[None, :])
    state = attend(ids[0], frame_bounds, [chunk], start, None, False)
    for s in range(1, 4):
        state = attend(
            jnp.concatenate(ids[2 * s - 1 : 2 * s + 1]),
            frame_bounds,
            [right[s], left[s]],
            start,
            state,
            False,
        )
    attended = attend(ids[7], frame_bounds, [right[4]], start, state, True)

    rel = [0, -1, 1, 2]
    gathered = jnp.concatenate(
        [attended] + [shift(attended, "x", -r) for r in rel[1:]], axis=0
    )
    core = core.astype(jnp.int32)[None]
    for_other = project(1 - core, gathered, weight)
    from_other = shift(for_other, "c", 1)
    for_own = project(core, gathered, weight)
    partial = (for_own + from_other).astype(jnp.bfloat16).reshape(512, 512)
    pieces = lax.all_to_all(partial, "yl", split_axis=0, concat_axis=0, tiled=True)
    combined = jnp.sum(pieces.reshape(4, TOK, 512).astype(jnp.float32), axis=0)
    result = (jnp.tanh(attn_gate[0]) * combined).astype(jnp.bfloat16)
    pairs = [
        (x * 4 + y, ((x + rel[y]) % 4) * 4 + x) for x in range(4) for y in range(4)
    ]
    return lax.ppermute(result, ("x", "yl"), pairs)


def solution(mesh):
    fine = Mesh(mesh.devices.reshape(4, 2, 8, 4, 2), ("x", "yh", "z", "yl", "c"))
    frame, group = ("x", "yh", "z"), ("yl", "c")
    placed = (
        P(frame, group),
        P(frame, group),
        P(frame, group),
        P(),
        P(None, frame),
        P(group, frame, None),
        P(),
    )
    return jax.shard_map(
        work, mesh=fine, in_specs=placed, out_specs=P(frame, group), check_vma=False
    )
```

```python
import math

import jax
import jax.numpy as jnp
from jax import lax
from jax.experimental import pallas as pl
from jax.experimental.pallas import tpu as pltpu
from jax.sharding import Mesh, PartitionSpec as P


D = 128
HEADS = 8
TOK = 128
ROWS = HEADS * TOK
BLOCKS = 4
WIDE = 256
PACK = TOK + 16
LOW = -1e30
EXP2_SCALE = math.log2(math.e) / math.sqrt(D)
VMEM = pl.BlockSpec(memory_space=pltpu.VMEM)
SMEM = pl.BlockSpec(memory_space=pltpu.SMEM)
FRAMES = ("x", "yh", "z")


def shift(value, axis, steps):
    count = lax.axis_size(axis)
    return lax.ppermute(value, axis, [(s, (s + steps) % count) for s in range(count)])


def attention_kernel(n_chunks, first, half, ids_ref, *refs):
    refs = list(refs)
    packs = [refs.pop(0) for _ in range(2)]
    chunks = [refs.pop(0) for _ in range(n_chunks)]
    if first:
        gain_ref = refs.pop(0)
    else:
        nq_ref, m_in, l_in, acc_in = [refs.pop(0) for _ in range(4)]
    if half is not None:
        out_ref = refs.pop(0)
    elif first:
        nq_ref, m_out, l_out, acc_out = [refs.pop(0) for _ in range(4)]
    else:
        m_out, l_out, acc_out = [refs.pop(0) for _ in range(3)]
    if first:
        for b, pack in enumerate(packs):
            for h in range(HEADS):
                x = pack[0:TOK, h * D : (h + 1) * D].astype(jnp.float32)
                mean = jnp.mean(x * x, axis=-1, keepdims=True)
                x = x * lax.rsqrt(mean + 1e-05) * gain_ref[...]
                at = b * ROWS + h * TOK
                nq_ref[at : at + TOK, :] = x.astype(jnp.bfloat16)
    limits = []
    for pack in packs:
        rows = pack[TOK:PACK, 0:TOK].astype(jnp.float32)
        rows = jnp.concatenate([rows] * (WIDE // TOK), axis=1)
        limits.append((rows[0:1], rows[1:2]))
    per = ROWS // WIDE
    ws = range(2 * per) if half is None else range(half * per, (half + 1) * per)
    cols = {w: slice(w * WIDE, (w + 1) * WIDE) for w in ws}
    if first:
        state = {
            w: (
                jnp.full((1, WIDE), LOW, jnp.float32),
                jnp.zeros((8, WIDE), jnp.float32),
                jnp.zeros((D, WIDE), jnp.float32),
            )
            for w in ws
        }
    else:
        state = {w: (m_in[:, cols[w]], l_in[:, cols[w]], acc_in[:, cols[w]]) for w in ws}
    units = [(c, w) for c in range(n_chunks) for w in ws]

    def score(unit):
        c, w = unit
        k = chunks[c][:, 0].reshape(BLOCKS * D, D)
        return lax.dot_general(
            k,
            nq_ref[cols[w], :],
            (((1,), (1,)), ((), ())),
            preferred_element_type=jnp.float32,
        )

    def soften(unit, s, m, l):
        c, w = unit
        lower, upper = limits[w // per]
        allowed = []
        new = m
        for j in range(BLOCKS):
            block = ids_ref[c * BLOCKS + j].astype(jnp.float32)
            ok = (lower <= block) & (block < upper)
            top = jnp.max(s[j * D : (j + 1) * D], axis=0, keepdims=True)
            new = jnp.maximum(new, jnp.where(ok, top, LOW))
            allowed.append(ok)
        factor = jnp.exp2((m - new) * EXP2_SCALE)
        l = l * factor
        parts = []
        for j in range(BLOCKS):
            base = jnp.where(allowed[j], new * EXP2_SCALE, -LOW)
            p = jnp.exp2(s[j * D : (j + 1) * D] * EXP2_SCALE - base)
            l = l + jnp.sum(p.reshape(D // 8, 8, WIDE), axis=0)
            parts.append(p.astype(jnp.bfloat16))
        return jnp.concatenate(parts, axis=0), new, l, factor

    def collect(unit, p, acc, factor):
        c, _ = unit
        v = chunks[c][:, 1].reshape(BLOCKS * D, D)
        return acc * factor + lax.dot_general(
            v, p, (((0,), (0,)), ((), ())), preferred_element_type=jnp.float32
        )

    ahead = score(units[0])
    pending = None
    for at, unit in enumerate(units):
        s = ahead
        if at + 1 < len(units):
            ahead = score(units[at + 1])
        w = unit[1]
        m, l, acc = state[w]
        p, m, l, factor = soften(unit, s, m, l)
        if pending is not None:
            u, p0, f0 = pending
            m0, l0, acc0 = state[u[1]]
            state[u[1]] = (m0, l0, collect(u, p0, acc0, f0))
        state[w] = (m, l, state[w][2])
        pending = (unit, p, factor)
    u, p0, f0 = pending
    m0, l0, acc0 = state[u[1]]
    state[u[1]] = (m0, l0, collect(u, p0, acc0, f0))

    for w in ws:
        m, l, acc = state[w]
        if half is not None:
            at = slice((w % per) * WIDE, (w % per + 1) * WIDE)
            out_ref[0:D, at] = acc
            out_ref[D : D + 8, at] = l
            out_ref[D + 8 : D + 16, at] = jnp.broadcast_to(m, (8, WIDE))
        else:
            m_out[:, cols[w]] = m
            l_out[:, cols[w]] = l
            acc_out[:, cols[w]] = acc


def attend(ids, packs, chunks, gain, state, half=None):
    first = state is None
    sums = (
        jax.ShapeDtypeStruct((1, 2 * ROWS), jnp.float32),
        jax.ShapeDtypeStruct((8, 2 * ROWS), jnp.float32),
        jax.ShapeDtypeStruct((D, 2 * ROWS), jnp.float32),
    )
    if half is not None:
        out_shape = jax.ShapeDtypeStruct((D + 16, ROWS), jnp.float32)
    elif first:
        out_shape = (jax.ShapeDtypeStruct((2 * ROWS, D), jnp.bfloat16),) + sums
    else:
        out_shape = sums
    extra = (gain,) if first else state
    n_keys = len(chunks) * BLOCKS * D
    rows = 2 * ROWS if half is None else ROWS

    def body(*refs):
        attention_kernel(len(chunks), first, half, *refs)

    out = pl.pallas_call(
        body,
        out_shape=out_shape,
        in_specs=[SMEM] + [VMEM] * (2 + len(chunks) + len(extra)),
        out_specs=VMEM if half is not None else (VMEM,) * len(out_shape),
        cost_estimate=pl.CostEstimate(
            flops=4 * rows * n_keys * D,
            bytes_accessed=n_keys * D * 4 + rows * D * 12,
            transcendentals=rows * n_keys,
        ),
        compiler_params=pltpu.CompilerParams(vmem_limit_bytes=40 << 20),
    )(ids, *packs, *chunks, *extra)
    if half is not None or first:
        return out
    return (state[0],) + tuple(out)


def merge_kernel(a_ref, b_ref, out_ref):
    a, b = a_ref[...], b_ref[...]
    top = jnp.maximum(a[D + 8 : D + 9], b[D + 8 : D + 9])
    fa = jnp.exp2((a[D + 8 : D + 9] - top) * EXP2_SCALE)
    fb = jnp.exp2((b[D + 8 : D + 9] - top) * EXP2_SCALE)
    total = jnp.sum(a[D : D + 8], axis=0, keepdims=True) * fa
    total = total + jnp.sum(b[D : D + 8], axis=0, keepdims=True) * fb
    o = (a[0:D] * fa + b[0:D] * fb) / total
    for h in range(HEADS):
        at = slice(h * TOK, (h + 1) * TOK)
        out_ref[:, at] = o[:, at].T.astype(jnp.bfloat16)


def merge(a, b):
    return pl.pallas_call(
        merge_kernel,
        out_shape=jax.ShapeDtypeStruct((TOK, ROWS), jnp.bfloat16),
        in_specs=[VMEM, VMEM],
        out_specs=VMEM,
        cost_estimate=pl.CostEstimate(
            flops=6 * ROWS * D, bytes_accessed=ROWS * D * 10, transcendentals=0
        ),
        compiler_params=pltpu.CompilerParams(vmem_limit_bytes=32 << 20),
    )(a, b)


def project_kernel(col_ref, core_ref, a0, a1, a2, a3, w_ref, out_ref):
    total = None
    a = jnp.concatenate([a0[...], a1[...], a2[...], a3[...]], axis=0)
    for x in range(4):
        w = jnp.concatenate([w_ref[:, 0, x], w_ref[:, 1, x]]).reshape(256, 512)
        part = jnp.dot(
            a[:, x * 256 : (x + 1) * 256], w, preferred_element_type=jnp.float32
        )
        total = part if total is None else total + part
    for k in range(4):
        out_ref[(core_ref[0] + k) % 4] = total[k * TOK : (k + 1) * TOK]


def project(column, core, slots, weight):
    return pl.pallas_call(
        project_kernel,
        grid_spec=pltpu.PrefetchScalarGridSpec(
            num_scalar_prefetch=2,
            grid=(1,),
            in_specs=[pl.BlockSpec((TOK, ROWS), lambda i, col, core: (0, 0))] * 4
            + [
                pl.BlockSpec(
                    (8, 2, 4, 16, 512), lambda i, col, core: (0, 0, 0, 0, col[0])
                ),
            ],
            out_specs=pl.BlockSpec((4, TOK, 512), lambda i, col, core: (0, 0, 0)),
        ),
        out_shape=jax.ShapeDtypeStruct((4, TOK, 512), jnp.float32),
        cost_estimate=pl.CostEstimate(
            flops=512 * 1024 * 1024, bytes_accessed=3 << 20, transcendentals=0
        ),
        compiler_params=pltpu.CompilerParams(vmem_limit_bytes=32 << 20),
    )(column, core, *slots, weight)


def work(queries, keys, values, q_gain, frame_bounds, output_weight, attn_gate):
    ax, ay, az = lax.axis_index("x"), lax.axis_index("yh"), lax.axis_index("z")
    core = lax.axis_index("c")

    def trade(value, di=0, dy=0):
        pairs = []
        for i in range(2):
            for y in range(2):
                for a in range(2):
                    for c in range(2):
                        source = ((2 * i + a) * 2 + y) * 2 + c
                        x = 2 * ((i + di) % 2) + c
                        pairs.append((source, (x * 2 + (y + dy) % 2) * 2 + a))
        return lax.ppermute(value, ("x", "yh", "c"), pairs)

    own = jnp.stack([keys, values])[None]
    chunk = jnp.concatenate(
        [trade(own), trade(own, di=1), trade(own, dy=1), trade(own, di=1, dy=1)]
    )
    block_x = 2 * (ax // 2) + core
    in_chunk = jnp.stack(
        [
            ((block_x + 2 * di) % 4) * 16 + ((ay + dy) % 2) * 8
            for dy in (0, 1)
            for di in (0, 1)
        ]
    ).astype(jnp.int32)
    hops = [0, -1, 1, -2, 2, -3, 3, -4]
    ids = [in_chunk + (az + h) % 8 for h in hops]

    bounds = jnp.pad(frame_bounds.astype(jnp.bfloat16), ((0, 14), (0, ROWS - TOK)))
    near = trade(jnp.concatenate([queries, bounds]))
    far = shift(near, "c", 1)
    packs = (near, far)

    quarter = output_weight[0].reshape(16, 4, 1024).transpose(1, 0, 2)
    quarter = lax.all_to_all(
        quarter.reshape(64, 1024), "x", split_axis=0, concat_axis=0, tiled=True
    )
    partner = shift(quarter, "yh", 1)
    both = jnp.stack(
        [jnp.where(ay == 0, quarter, partner), jnp.where(ay == 0, partner, quarter)]
    )
    weight = lax.all_gather(both.reshape(128, 1024), "z", axis=0, tiled=True)
    weight = weight.reshape(8, 2, 4, 16, 1024)

    right, left = [chunk], [chunk]
    for s in range(1, 5):
        right.append(shift(right[-1], "z", 1))
        if s < 4:
            left.append(shift(left[-1], "z", -1))
    gain = q_gain[None, :]
    state = attend(ids[0], packs, [chunk], gain, None)
    for s in range(1, 4):
        state = attend(
            jnp.concatenate(ids[2 * s - 1 : 2 * s + 1]),
            packs,
            [right[s], left[s]],
            gain,
            state,
        )
    send = attend(ids[7], packs, [right[4]], gain, state, half=1)
    received = shift(send, "c", 1)
    keep = attend(ids[7], packs, [right[4]], gain, state, half=0)
    attended = merge(keep, received)

    slots = []
    for k in range(4):
        pairs = [
            (x * 2 + c, ((x + k + c) % 4) * 2 + x % 2) for x in range(4) for c in range(2)
        ]
        slots.append(lax.ppermute(attended, ("x", "c"), pairs))
    core = core.astype(jnp.int32)[None]
    for_other = project(1 - core, core, slots, weight)
    from_other = shift(for_other, "c", 1)
    for_own = project(core, core, slots, weight)
    partial = (for_own + from_other).astype(jnp.bfloat16).reshape(512, 512)
    pieces = lax.all_to_all(partial, "yl", split_axis=0, concat_axis=0, tiled=True)
    combined = jnp.sum(pieces.reshape(4, TOK, 512).astype(jnp.float32), axis=0)
    result = (jnp.tanh(attn_gate[0]) * combined).astype(jnp.bfloat16)
    pairs = [(x * 4 + y, ((x - y) % 4) * 4 + x) for x in range(4) for y in range(4)]
    return lax.ppermute(result, ("x", "yl"), pairs)


def solution(mesh):
    fine = Mesh(mesh.devices.reshape(4, 2, 8, 4, 2), ("x", "yh", "z", "yl", "c"))
    group = ("yl", "c")
    placed = (
        P(FRAMES, group),
        P(FRAMES, group),
        P(FRAMES, group),
        P(),
        P(None, FRAMES),
        P(group, FRAMES, None),
        P(),
    )
    return jax.shard_map(
        work, mesh=fine, in_specs=placed, out_specs=P(FRAMES, group), check_vma=False
    )
```

```python
import math

import jax
import jax.numpy as jnp
from jax import lax
from jax.experimental import pallas as pl
from jax.experimental.pallas import tpu as pltpu
from jax.sharding import Mesh, PartitionSpec as P


D = 128
HEADS = 8
TOK = 128
ROWS = HEADS * TOK
BLOCKS = 4
WIDE = 256
PACK = TOK + 16
LOW = -1e30
EXP2_SCALE = math.log2(math.e) / math.sqrt(D)
VMEM = pl.BlockSpec(memory_space=pltpu.VMEM)
SMEM = pl.BlockSpec(memory_space=pltpu.SMEM)
FRAMES = ("x", "yh", "z")


def shift(value, axis, steps):
    count = lax.axis_size(axis)
    return lax.ppermute(value, axis, [(s, (s + steps) % count) for s in range(count)])


def attention_kernel(n_chunks, first, half, ids_ref, *refs):
    refs = list(refs)
    packs = [refs.pop(0) for _ in range(2)]
    chunks = [refs.pop(0) for _ in range(n_chunks)]
    if first:
        gain_ref = refs.pop(0)
    else:
        nq_ref, m_in, l_in, acc_in = [refs.pop(0) for _ in range(4)]
    if half is not None:
        out_ref = refs.pop(0)
    elif first:
        nq_ref, m_out, l_out, acc_out = [refs.pop(0) for _ in range(4)]
    else:
        m_out, l_out, acc_out = [refs.pop(0) for _ in range(3)]
    if first:
        for b, pack in enumerate(packs):
            for h in range(HEADS):
                x = pack[0:TOK, h * D : (h + 1) * D].astype(jnp.float32)
                mean = jnp.mean(x * x, axis=-1, keepdims=True)
                x = x * lax.rsqrt(mean + 1e-05) * gain_ref[...]
                at = b * ROWS + h * TOK
                nq_ref[at : at + TOK, :] = x.astype(jnp.bfloat16)
    limits = []
    for pack in packs:
        rows = pack[TOK:PACK, 0:TOK].astype(jnp.float32)
        rows = jnp.concatenate([rows] * (WIDE // TOK), axis=1)
        limits.append((rows[0:1], rows[1:2]))
    per = ROWS // WIDE
    ws = range(2 * per) if half is None else range(half * per, (half + 1) * per)
    cols = {w: slice(w * WIDE, (w + 1) * WIDE) for w in ws}
    if first:
        state = {
            w: (
                jnp.full((1, WIDE), LOW, jnp.float32),
                jnp.zeros((8, WIDE), jnp.float32),
                jnp.zeros((D, WIDE), jnp.float32),
            )
            for w in ws
        }
    else:
        state = {w: (m_in[:, cols[w]], l_in[:, cols[w]], acc_in[:, cols[w]]) for w in ws}
    units = [(c, w) for c in range(n_chunks) for w in ws]

    def score(unit):
        c, w = unit
        k = chunks[c][0:BLOCKS, 0].reshape(BLOCKS * D, D)
        return lax.dot_general(
            k,
            nq_ref[cols[w], :],
            (((1,), (1,)), ((), ())),
            preferred_element_type=jnp.float32,
        )

    def soften(unit, s, m, l):
        c, w = unit
        lower, upper = limits[w // per]
        allowed = []
        new = m
        for j in range(BLOCKS):
            block = ids_ref[c * BLOCKS + j].astype(jnp.float32)
            ok = (lower <= block) & (block < upper)
            top = jnp.max(s[j * D : (j + 1) * D], axis=0, keepdims=True)
            new = jnp.maximum(new, jnp.where(ok, top, LOW))
            allowed.append(ok)
        factor = jnp.exp2((m - new) * EXP2_SCALE)
        l = l * factor
        parts = []
        for j in range(BLOCKS):
            base = jnp.where(allowed[j], new * EXP2_SCALE, -LOW)
            p = jnp.exp2(s[j * D : (j + 1) * D] * EXP2_SCALE - base)
            l = l + jnp.sum(p.reshape(D // 8, 8, WIDE), axis=0)
            parts.append(p.astype(jnp.bfloat16))
        return jnp.concatenate(parts, axis=0), new, l, factor

    def collect(unit, p, acc, factor):
        c, _ = unit
        v = chunks[c][0:BLOCKS, 1].reshape(BLOCKS * D, D)
        return acc * factor + lax.dot_general(
            v, p, (((0,), (0,)), ((), ())), preferred_element_type=jnp.float32
        )

    ahead = score(units[0])
    pending = None
    for at, unit in enumerate(units):
        s = ahead
        if at + 1 < len(units):
            ahead = score(units[at + 1])
        w = unit[1]
        m, l, acc = state[w]
        p, m, l, factor = soften(unit, s, m, l)
        if pending is not None:
            u, p0, f0 = pending
            m0, l0, acc0 = state[u[1]]
            state[u[1]] = (m0, l0, collect(u, p0, acc0, f0))
        state[w] = (m, l, state[w][2])
        pending = (unit, p, factor)
    u, p0, f0 = pending
    m0, l0, acc0 = state[u[1]]
    state[u[1]] = (m0, l0, collect(u, p0, acc0, f0))

    for w in ws:
        m, l, acc = state[w]
        if half is not None:
            at = slice((w % per) * WIDE, (w % per + 1) * WIDE)
            out_ref[0:D, at] = acc
            out_ref[D : D + 8, at] = l
            out_ref[D + 8 : D + 16, at] = jnp.broadcast_to(m, (8, WIDE))
        else:
            m_out[:, cols[w]] = m
            l_out[:, cols[w]] = l
            acc_out[:, cols[w]] = acc


def attend(ids, packs, chunks, gain, state, half=None):
    first = state is None
    sums = (
        jax.ShapeDtypeStruct((1, 2 * ROWS), jnp.float32),
        jax.ShapeDtypeStruct((8, 2 * ROWS), jnp.float32),
        jax.ShapeDtypeStruct((D, 2 * ROWS), jnp.float32),
    )
    if half is not None:
        out_shape = jax.ShapeDtypeStruct((D + 16, ROWS), jnp.float32)
    elif first:
        out_shape = (jax.ShapeDtypeStruct((2 * ROWS, D), jnp.bfloat16),) + sums
    else:
        out_shape = sums
    extra = (gain,) if first else state
    n_keys = len(chunks) * BLOCKS * D
    rows = 2 * ROWS if half is None else ROWS

    def body(*refs):
        attention_kernel(len(chunks), first, half, *refs)

    out = pl.pallas_call(
        body,
        out_shape=out_shape,
        in_specs=[SMEM] + [VMEM] * (2 + len(chunks) + len(extra)),
        out_specs=VMEM if half is not None else (VMEM,) * len(out_shape),
        cost_estimate=pl.CostEstimate(
            flops=4 * rows * n_keys * D,
            bytes_accessed=n_keys * D * 4 + rows * D * 12,
            transcendentals=rows * n_keys,
        ),
        compiler_params=pltpu.CompilerParams(vmem_limit_bytes=16 << 20),
    )(ids, *packs, *chunks, *extra)
    if half is not None or first:
        return out
    return (state[0],) + tuple(out)


def merge_kernel(a_ref, b_ref, out_ref):
    a, b = a_ref[...], b_ref[...]
    top = jnp.maximum(a[D + 8 : D + 9], b[D + 8 : D + 9])
    fa = jnp.exp2((a[D + 8 : D + 9] - top) * EXP2_SCALE)
    fb = jnp.exp2((b[D + 8 : D + 9] - top) * EXP2_SCALE)
    total = jnp.sum(a[D : D + 8], axis=0, keepdims=True) * fa
    total = total + jnp.sum(b[D : D + 8], axis=0, keepdims=True) * fb
    o = (a[0:D] * fa + b[0:D] * fb) / total
    for h in range(HEADS):
        at = slice(h * TOK, (h + 1) * TOK)
        out_ref[:, at] = o[:, at].T.astype(jnp.bfloat16)


def merge(a, b):
    return pl.pallas_call(
        merge_kernel,
        out_shape=jax.ShapeDtypeStruct((TOK, ROWS), jnp.bfloat16),
        in_specs=[VMEM, VMEM],
        out_specs=VMEM,
        cost_estimate=pl.CostEstimate(
            flops=6 * ROWS * D, bytes_accessed=ROWS * D * 10, transcendentals=0
        ),
        compiler_params=pltpu.CompilerParams(vmem_limit_bytes=16 << 20),
    )(a, b)


def assemble_kernel(at_ref, *refs):
    chunks, first_ref, second_ref, out_ref = refs[:8], refs[8], refs[9], refs[10]
    for p in range(8):
        for y in range(2):
            if y == 0:
                source, base = chunks[p], BLOCKS
            elif p < 5:
                source, base = first_ref, 2 * p
            else:
                source, base = second_ref, 2 * (p - 5)
            slot = at_ref[2 * p + y]
            for x in range(4):
                block = source[base + x // 2, x % 2]
                for t in range(8):
                    out_ref[x, slot, :, t * 128 : (t + 1) * 128] = block[
                        t * 16 : (t + 1) * 16
                    ]


def assemble(at, chunks, first, second):
    return pl.pallas_call(
        assemble_kernel,
        out_shape=jax.ShapeDtypeStruct((4, 16, 16, 1024), jnp.bfloat16),
        in_specs=[SMEM] + [VMEM] * 10,
        out_specs=VMEM,
        cost_estimate=pl.CostEstimate(
            flops=0, bytes_accessed=4 << 20, transcendentals=0
        ),
        compiler_params=pltpu.CompilerParams(vmem_limit_bytes=16 << 20),
    )(at, *chunks, first, second)


def project_kernel(col_ref, turn_ref, a0, a1, a2, a3, w_ref, out_ref):
    total = None
    a = jnp.concatenate([a0[...], a1[...], a2[...], a3[...]], axis=0)
    for x in range(4):
        part = jnp.dot(
            a[:, x * 256 : (x + 1) * 256],
            w_ref[x].reshape(256, 512),
            preferred_element_type=jnp.float32,
        )
        total = part if total is None else total + part
    for k in range(4):
        out_ref[(turn_ref[0] + k) % 4] = total[k * TOK : (k + 1) * TOK]


def project(column, turn, slots, weight):
    return pl.pallas_call(
        project_kernel,
        grid_spec=pltpu.PrefetchScalarGridSpec(
            num_scalar_prefetch=2,
            grid=(1,),
            in_specs=[pl.BlockSpec((TOK, ROWS), lambda i, col, turn: (0, 0))] * 4
            + [
                pl.BlockSpec((4, 16, 16, 512), lambda i, col, turn: (0, 0, 0, col[0])),
            ],
            out_specs=pl.BlockSpec((4, TOK, 512), lambda i, col, turn: (0, 0, 0)),
        ),
        out_shape=jax.ShapeDtypeStruct((4, TOK, 512), jnp.float32),
        cost_estimate=pl.CostEstimate(
            flops=512 * 1024 * 1024, bytes_accessed=3 << 20, transcendentals=0
        ),
        compiler_params=pltpu.CompilerParams(vmem_limit_bytes=16 << 20),
    )(column, turn, *slots, weight)


def work(queries, keys, values, q_gain, frame_bounds, output_weight, attn_gate):
    ax, ay, az = lax.axis_index("x"), lax.axis_index("yh"), lax.axis_index("z")
    core = lax.axis_index("c")

    def trade(value, di=0, dy=0):
        pairs = []
        for i in range(2):
            for y in range(2):
                for a in range(2):
                    for c in range(2):
                        source = ((2 * i + a) * 2 + y) * 2 + c
                        x = 2 * ((i + di) % 2) + c
                        pairs.append((source, (x * 2 + (y + dy) % 2) * 2 + a))
        return lax.ppermute(value, ("x", "yh", "c"), pairs)

    quarter = output_weight[0].reshape(16, 4, 8, 128).transpose(1, 2, 0, 3)
    quarter = lax.all_to_all(
        quarter.reshape(512, 128), "x", split_axis=0, concat_axis=0, tiled=True
    )
    own = jnp.stack([keys, values])[None]
    chunk = jnp.concatenate(
        [
            trade(own),
            trade(own, di=1),
            trade(own, dy=1),
            trade(own, di=1, dy=1),
            quarter.reshape(2, 2, 128, 128),
        ]
    )
    block_x = 2 * (ax // 2) + core
    in_chunk = jnp.stack(
        [
            ((block_x + 2 * di) % 4) * 16 + ((ay + dy) % 2) * 8
            for dy in (0, 1)
            for di in (0, 1)
        ]
    ).astype(jnp.int32)
    hops = [0, -1, 1, -2, 2, -3, 3, -4]
    ids = [in_chunk + (az + h) % 8 for h in hops]

    bounds = jnp.pad(frame_bounds.astype(jnp.bfloat16), ((0, 14), (0, ROWS - TOK)))
    near = trade(jnp.concatenate([queries, bounds]))
    far = shift(near, "c", 1)
    packs = (near, far)

    right, left = [chunk], [chunk]
    for s in range(1, 5):
        right.append(shift(right[-1], "z", 1))
        if s < 4:
            left.append(shift(left[-1], "z", -1))
    gain = q_gain[None, :]
    state = attend(ids[0], packs, [chunk], gain, None)
    for s in range(1, 4):
        state = attend(
            jnp.concatenate(ids[2 * s - 1 : 2 * s + 1]),
            packs,
            [right[s], left[s]],
            gain,
            state,
        )
    send = attend(ids[7], packs, [right[4]], gain, state, half=1)
    received = shift(send, "c", 1)
    keep = attend(ids[7], packs, [right[4]], gain, state, half=0)
    attended = merge(keep, received)

    slots = []
    for k in range(4):
        pairs = [
            (x * 2 + c, ((x + k + c) % 4) * 2 + x % 2) for x in range(4) for c in range(2)
        ]
        slots.append(lax.ppermute(attended, ("x", "c"), pairs))
    parts = [chunk, right[1], left[1], right[2], left[2], right[3], left[3], right[4]]
    first = shift(jnp.concatenate([c[BLOCKS:] for c in parts[:5]]), "yh", 1)
    second = shift(jnp.concatenate([c[BLOCKS:] for c in parts[5:]]), "yh", 1)
    at = jnp.stack(
        [((ay + dy) % 2) * 8 + (az + h) % 8 for h in hops for dy in (0, 1)]
    ).astype(jnp.int32)
    weight = assemble(at, parts, first, second)

    core = core.astype(jnp.int32)[None]
    turn = (core + 4 - lax.axis_index("yl")) % 4
    for_other = project(1 - core, turn, slots, weight)
    from_other = shift(for_other, "c", 1)
    for_own = project(core, turn, slots, weight)
    combined = None
    for s in range(4):
        pairs = [
            (x * 4 + y, ((x - y - s) % 4) * 4 + x) for x in range(4) for y in range(4)
        ]
        part = (for_own[s] + from_other[s]).astype(jnp.bfloat16)
        part = lax.ppermute(part, ("x", "yl"), pairs).astype(jnp.float32)
        combined = part if combined is None else combined + part
    return (jnp.tanh(attn_gate[0]) * combined).astype(jnp.bfloat16)


def solution(mesh):
    fine = Mesh(mesh.devices.reshape(4, 2, 8, 4, 2), ("x", "yh", "z", "yl", "c"))
    group = ("yl", "c")
    placed = (
        P(FRAMES, group),
        P(FRAMES, group),
        P(FRAMES, group),
        P(),
        P(None, FRAMES),
        P(group, FRAMES, None),
        P(),
    )
    return jax.shard_map(
        work, mesh=fine, in_specs=placed, out_specs=P(FRAMES, group), check_vma=False
    )
```

```python
import math

import jax
import jax.numpy as jnp
from jax import lax
from jax.experimental import pallas as pl
from jax.experimental.pallas import tpu as pltpu
from jax.sharding import Mesh, PartitionSpec as P


D = 128
HEADS = 8
TOK = 128
ROWS = HEADS * TOK
BLOCKS = 4
WIDE = 256
PACK = TOK + 16
LOW = -1e30
EXP2_SCALE = math.log2(math.e) / math.sqrt(D)
VMEM = pl.BlockSpec(memory_space=pltpu.VMEM)
SMEM = pl.BlockSpec(memory_space=pltpu.SMEM)
FRAMES = ("x", "yh", "z")


def shift(value, axis, steps):
    count = lax.axis_size(axis)
    return lax.ppermute(value, axis, [(s, (s + steps) % count) for s in range(count)])


def attention_kernel(n_chunks, first, half, ids_ref, *refs):
    refs = list(refs)
    packs = [refs.pop(0) for _ in range(2)]
    chunks = [refs.pop(0) for _ in range(n_chunks)]
    if first:
        gain_ref = refs.pop(0)
    else:
        nq_ref, m_in, l_in, acc_in = [refs.pop(0) for _ in range(4)]
    if half is not None:
        out_ref = refs.pop(0)
    elif first:
        nq_ref, m_out, l_out, acc_out = [refs.pop(0) for _ in range(4)]
    else:
        m_out, l_out, acc_out = [refs.pop(0) for _ in range(3)]
    if first:
        for b, pack in enumerate(packs):
            for h in range(HEADS):
                x = pack[0:TOK, h * D : (h + 1) * D].astype(jnp.float32)
                mean = jnp.mean(x * x, axis=-1, keepdims=True)
                x = x * lax.rsqrt(mean + 1e-05) * gain_ref[...]
                at = b * ROWS + h * TOK
                nq_ref[at : at + TOK, :] = x.astype(jnp.bfloat16)
    limits = []
    for pack in packs:
        rows = pack[TOK:PACK, 0:TOK].astype(jnp.float32)
        rows = jnp.concatenate([rows] * (WIDE // TOK), axis=1)
        limits.append((rows[0:1], rows[1:2]))
    per = ROWS // WIDE
    ws = range(2 * per) if half is None else range(half * per, (half + 1) * per)
    cols = {w: slice(w * WIDE, (w + 1) * WIDE) for w in ws}
    if first:
        state = {
            w: (
                jnp.full((1, WIDE), LOW, jnp.float32),
                jnp.zeros((8, WIDE), jnp.float32),
                jnp.zeros((D, WIDE), jnp.float32),
            )
            for w in ws
        }
    else:
        state = {w: (m_in[:, cols[w]], l_in[:, cols[w]], acc_in[:, cols[w]]) for w in ws}
    units = [(c, w) for c in range(n_chunks) for w in ws]

    def score(unit):
        c, w = unit
        k = chunks[c][0:BLOCKS, 0].reshape(BLOCKS * D, D)
        return lax.dot_general(
            k,
            nq_ref[cols[w], :],
            (((1,), (1,)), ((), ())),
            preferred_element_type=jnp.float32,
        )

    def soften(unit, s, m, l):
        c, w = unit
        lower, upper = limits[w // per]
        allowed = []
        new = m
        for j in range(BLOCKS):
            block = ids_ref[c * BLOCKS + j].astype(jnp.float32)
            ok = (lower <= block) & (block < upper)
            top = jnp.max(s[j * D : (j + 1) * D], axis=0, keepdims=True)
            new = jnp.maximum(new, jnp.where(ok, top, LOW))
            allowed.append(ok)
        factor = jnp.exp2((m - new) * EXP2_SCALE)
        l = l * factor
        parts = []
        for j in range(BLOCKS):
            base = jnp.where(allowed[j], new * EXP2_SCALE, -LOW)
            p = jnp.exp2(s[j * D : (j + 1) * D] * EXP2_SCALE - base)
            l = l + jnp.sum(p.reshape(D // 8, 8, WIDE), axis=0)
            parts.append(p.astype(jnp.bfloat16))
        return jnp.concatenate(parts, axis=0), new, l, factor

    def collect(unit, p, acc, factor):
        c, _ = unit
        v = chunks[c][0:BLOCKS, 1].reshape(BLOCKS * D, D)
        return acc * factor + lax.dot_general(
            v, p, (((0,), (0,)), ((), ())), preferred_element_type=jnp.float32
        )

    ahead = score(units[0])
    pending = None
    for at, unit in enumerate(units):
        s = ahead
        if at + 1 < len(units):
            ahead = score(units[at + 1])
        w = unit[1]
        m, l, acc = state[w]
        p, m, l, factor = soften(unit, s, m, l)
        if pending is not None:
            u, p0, f0 = pending
            m0, l0, acc0 = state[u[1]]
            state[u[1]] = (m0, l0, collect(u, p0, acc0, f0))
        state[w] = (m, l, state[w][2])
        pending = (unit, p, factor)
    u, p0, f0 = pending
    m0, l0, acc0 = state[u[1]]
    state[u[1]] = (m0, l0, collect(u, p0, acc0, f0))

    for w in ws:
        m, l, acc = state[w]
        if half is not None:
            at = slice((w % per) * WIDE, (w % per + 1) * WIDE)
            out_ref[0:D, at] = acc
            out_ref[D : D + 8, at] = l
            out_ref[D + 8 : D + 16, at] = jnp.broadcast_to(m, (8, WIDE))
        else:
            m_out[:, cols[w]] = m
            l_out[:, cols[w]] = l
            acc_out[:, cols[w]] = acc


def attend(ids, packs, chunks, gain, state, half=None):
    first = state is None
    sums = (
        jax.ShapeDtypeStruct((1, 2 * ROWS), jnp.float32),
        jax.ShapeDtypeStruct((8, 2 * ROWS), jnp.float32),
        jax.ShapeDtypeStruct((D, 2 * ROWS), jnp.float32),
    )
    if half is not None:
        out_shape = jax.ShapeDtypeStruct((D + 16, ROWS), jnp.float32)
    elif first:
        out_shape = (jax.ShapeDtypeStruct((2 * ROWS, D), jnp.bfloat16),) + sums
    else:
        out_shape = sums
    extra = (gain,) if first else state
    n_keys = len(chunks) * BLOCKS * D
    rows = 2 * ROWS if half is None else ROWS

    def body(*refs):
        attention_kernel(len(chunks), first, half, *refs)

    out = pl.pallas_call(
        body,
        out_shape=out_shape,
        in_specs=[SMEM] + [VMEM] * (2 + len(chunks) + len(extra)),
        out_specs=VMEM if half is not None else (VMEM,) * len(out_shape),
        cost_estimate=pl.CostEstimate(
            flops=4 * rows * n_keys * D,
            bytes_accessed=n_keys * D * 4 + rows * D * 12,
            transcendentals=rows * n_keys,
        ),
        compiler_params=pltpu.CompilerParams(vmem_limit_bytes=16 << 20),
    )(ids, *packs, *chunks, *extra)
    if half is not None or first:
        return out
    return (state[0],) + tuple(out)


def merge_kernel(a_ref, b_ref, out_ref):
    a, b = a_ref[...], b_ref[...]
    top = jnp.maximum(a[D + 8 : D + 9], b[D + 8 : D + 9])
    fa = jnp.exp2((a[D + 8 : D + 9] - top) * EXP2_SCALE)
    fb = jnp.exp2((b[D + 8 : D + 9] - top) * EXP2_SCALE)
    total = jnp.sum(a[D : D + 8], axis=0, keepdims=True) * fa
    total = total + jnp.sum(b[D : D + 8], axis=0, keepdims=True) * fb
    o = (a[0:D] * fa + b[0:D] * fb) / total
    for h in range(HEADS):
        at = slice(h * TOK, (h + 1) * TOK)
        out_ref[:, at] = o[:, at].T.astype(jnp.bfloat16)


def merge(a, b):
    return pl.pallas_call(
        merge_kernel,
        out_shape=jax.ShapeDtypeStruct((TOK, ROWS), jnp.bfloat16),
        in_specs=[VMEM, VMEM],
        out_specs=VMEM,
        cost_estimate=pl.CostEstimate(
            flops=6 * ROWS * D, bytes_accessed=ROWS * D * 10, transcendentals=0
        ),
        compiler_params=pltpu.CompilerParams(vmem_limit_bytes=16 << 20),
    )(a, b)


def assemble_kernel(at_ref, *refs):
    chunks, out_ref = refs[:8], refs[8]
    for p in range(8):
        for y in range(2):
            for x in range(4):
                tile = x * 2 + y
                block = chunks[p][BLOCKS + tile // 2, tile % 2]
                for t in range(8):
                    out_ref[x, y * 8 + at_ref[p], :, t * 128 : (t + 1) * 128] = block[
                        t * 16 : (t + 1) * 16
                    ]


def assemble(at, chunks):
    return pl.pallas_call(
        assemble_kernel,
        out_shape=jax.ShapeDtypeStruct((4, 16, 16, 1024), jnp.bfloat16),
        in_specs=[SMEM] + [VMEM] * 8,
        out_specs=VMEM,
        cost_estimate=pl.CostEstimate(
            flops=0, bytes_accessed=4 << 20, transcendentals=0
        ),
        compiler_params=pltpu.CompilerParams(vmem_limit_bytes=16 << 20),
    )(at, *chunks)


def project_kernel(col_ref, turn_ref, a0, a1, a2, a3, w_ref, out_ref):
    total = None
    a = jnp.concatenate([a0[...], a1[...], a2[...], a3[...]], axis=0)
    for x in range(4):
        part = jnp.dot(
            a[:, x * 256 : (x + 1) * 256],
            w_ref[x].reshape(256, 512),
            preferred_element_type=jnp.float32,
        )
        total = part if total is None else total + part
    for k in range(4):
        out_ref[(turn_ref[0] + k) % 4] = total[k * TOK : (k + 1) * TOK]


def project(column, turn, slots, weight):
    return pl.pallas_call(
        project_kernel,
        grid_spec=pltpu.PrefetchScalarGridSpec(
            num_scalar_prefetch=2,
            grid=(1,),
            in_specs=[pl.BlockSpec((TOK, ROWS), lambda i, col, turn: (0, 0))] * 4
            + [
                pl.BlockSpec((4, 16, 16, 512), lambda i, col, turn: (0, 0, 0, col[0])),
            ],
            out_specs=pl.BlockSpec((4, TOK, 512), lambda i, col, turn: (0, 0, 0)),
        ),
        out_shape=jax.ShapeDtypeStruct((4, TOK, 512), jnp.float32),
        cost_estimate=pl.CostEstimate(
            flops=512 * 1024 * 1024, bytes_accessed=3 << 20, transcendentals=0
        ),
        compiler_params=pltpu.CompilerParams(vmem_limit_bytes=16 << 20),
    )(column, turn, *slots, weight)


def work(queries, keys, values, q_gain, frame_bounds, output_weight, attn_gate):
    ax, ay, az = lax.axis_index("x"), lax.axis_index("yh"), lax.axis_index("z")
    core = lax.axis_index("c")

    def trade(value, di=0, dy=0):
        pairs = []
        for i in range(2):
            for y in range(2):
                for a in range(2):
                    for c in range(2):
                        source = ((2 * i + a) * 2 + y) * 2 + c
                        x = 2 * ((i + di) % 2) + c
                        pairs.append((source, (x * 2 + (y + dy) % 2) * 2 + a))
        return lax.ppermute(value, ("x", "yh", "c"), pairs)

    quarter = output_weight[0].reshape(16, 4, 1, 8, 128).transpose(1, 2, 3, 0, 4)
    quarter = jnp.broadcast_to(quarter, (4, 2, 8, 16, 128)).reshape(1024, 128)
    quarter = lax.all_to_all(
        quarter, ("x", "yh"), split_axis=0, concat_axis=0, tiled=True
    )
    own = jnp.stack([keys, values])[None]
    chunk = jnp.concatenate(
        [
            trade(own),
            trade(own, di=1),
            trade(own, dy=1),
            trade(own, di=1, dy=1),
            quarter.reshape(4, 2, 128, 128),
        ]
    )
    block_x = 2 * (ax // 2) + core
    in_chunk = jnp.stack(
        [
            ((block_x + 2 * di) % 4) * 16 + ((ay + dy) % 2) * 8
            for dy in (0, 1)
            for di in (0, 1)
        ]
    ).astype(jnp.int32)
    hops = [0, -1, 1, -2, 2, -3, 3, -4]
    ids = [in_chunk + (az + h) % 8 for h in hops]

    bounds = jnp.pad(frame_bounds.astype(jnp.bfloat16), ((0, 14), (0, ROWS - TOK)))
    near = trade(jnp.concatenate([queries, bounds]))
    far = shift(near, "c", 1)
    packs = (near, far)

    right, left = [chunk], [chunk]
    for s in range(1, 5):
        right.append(shift(right[-1], "z", 1))
        if s < 4:
            left.append(shift(left[-1], "z", -1))
    gain = q_gain[None, :]
    state = attend(ids[0], packs, [chunk], gain, None)
    for s in range(1, 4):
        state = attend(
            jnp.concatenate(ids[2 * s - 1 : 2 * s + 1]),
            packs,
            [right[s], left[s]],
            gain,
            state,
        )
    send = attend(ids[7], packs, [right[4]], gain, state, half=1)
    received = shift(send, "c", 1)
    keep = attend(ids[7], packs, [right[4]], gain, state, half=0)
    attended = merge(keep, received)

    slots = []
    for k in range(4):
        pairs = [
            (x * 2 + c, ((x + k + c) % 4) * 2 + x % 2) for x in range(4) for c in range(2)
        ]
        slots.append(lax.ppermute(attended, ("x", "c"), pairs))
    parts = [chunk, right[1], left[1], right[2], left[2], right[3], left[3], right[4]]
    at = jnp.stack([(az + h) % 8 for h in hops]).astype(jnp.int32)
    weight = assemble(at, parts)

    core = core.astype(jnp.int32)[None]
    turn = (core + 4 - lax.axis_index("yl")) % 4
    for_other = project(1 - core, turn, slots, weight)
    from_other = shift(for_other, "c", 1)
    for_own = project(core, turn, slots, weight)
    combined = for_own[0] + from_other[0]
    for s in range(1, 4):
        part = (for_own[s] + from_other[s]).astype(jnp.bfloat16)
        combined = combined + shift(part, "yl", s).astype(jnp.float32)
    result = (jnp.tanh(attn_gate[0]) * combined).astype(jnp.bfloat16)
    pairs = [(x * 4 + y, ((x - y) % 4) * 4 + x) for x in range(4) for y in range(4)]
    return lax.ppermute(result, ("x", "yl"), pairs)


def solution(mesh):
    fine = Mesh(mesh.devices.reshape(4, 2, 8, 4, 2), ("x", "yh", "z", "yl", "c"))
    group = ("yl", "c")
    placed = (
        P(FRAMES, group),
        P(FRAMES, group),
        P(FRAMES, group),
        P(),
        P(None, FRAMES),
        P(group, FRAMES, None),
        P(),
    )
    return jax.shard_map(
        work, mesh=fine, in_specs=placed, out_specs=P(FRAMES, group), check_vma=False
    )
```

```python
import math

import jax
import jax.numpy as jnp
from jax import lax
from jax.experimental import pallas as pl
from jax.experimental.pallas import tpu as pltpu
from jax.sharding import Mesh, PartitionSpec as P


D = 128
HEADS = 8
TOK = 128
ROWS = HEADS * TOK
BLOCKS = 4
WIDE = 256
PACK = TOK + 16
LOW = -1e30
EXP2_SCALE = math.log2(math.e) / math.sqrt(D)
VMEM = pl.BlockSpec(memory_space=pltpu.VMEM)
SMEM = pl.BlockSpec(memory_space=pltpu.SMEM)
FRAMES = ("x", "yh", "z")


def shift(value, axis, steps):
    count = lax.axis_size(axis)
    return lax.ppermute(value, axis, [(s, (s + steps) % count) for s in range(count)])


def attention_kernel(n_chunks, first, half, ids_ref, *refs):
    refs = list(refs)
    packs = [refs.pop(0) for _ in range(2)]
    chunks = [refs.pop(0) for _ in range(n_chunks)]
    if first:
        gain_ref = refs.pop(0)
    else:
        nq_ref, m_in, l_in, acc_in = [refs.pop(0) for _ in range(4)]
    if half is not None:
        out_ref = refs.pop(0)
    elif first:
        nq_ref, m_out, l_out, acc_out = [refs.pop(0) for _ in range(4)]
    else:
        m_out, l_out, acc_out = [refs.pop(0) for _ in range(3)]
    if first:
        for b, pack in enumerate(packs):
            for h in range(HEADS):
                x = pack[0:TOK, h * D : (h + 1) * D].astype(jnp.float32)
                mean = jnp.mean(x * x, axis=-1, keepdims=True)
                x = x * lax.rsqrt(mean + 1e-05) * gain_ref[...]
                at = b * ROWS + h * TOK
                nq_ref[at : at + TOK, :] = x.astype(jnp.bfloat16)
    limits = []
    for pack in packs:
        rows = pack[TOK:PACK, 0:TOK].astype(jnp.float32)
        rows = jnp.concatenate([rows] * (WIDE // TOK), axis=1)
        limits.append((rows[0:1], rows[1:2]))
    per = ROWS // WIDE
    ws = range(2 * per) if half is None else range(half * per, (half + 1) * per)
    cols = {w: slice(w * WIDE, (w + 1) * WIDE) for w in ws}
    if first:
        state = {
            w: (
                jnp.full((1, WIDE), LOW, jnp.float32),
                jnp.zeros((8, WIDE), jnp.float32),
                jnp.zeros((D, WIDE), jnp.float32),
            )
            for w in ws
        }
    else:
        state = {w: (m_in[:, cols[w]], l_in[:, cols[w]], acc_in[:, cols[w]]) for w in ws}
    units = [(c, w) for c in range(n_chunks) for w in ws]

    def score(unit):
        c, w = unit
        k = chunks[c][0:BLOCKS, 0].reshape(BLOCKS * D, D)
        return lax.dot_general(
            k,
            nq_ref[cols[w], :],
            (((1,), (1,)), ((), ())),
            preferred_element_type=jnp.float32,
        )

    def soften(unit, s, m, l):
        c, w = unit
        lower, upper = limits[w // per]
        allowed = []
        new = m
        for j in range(BLOCKS):
            block = ids_ref[c * BLOCKS + j].astype(jnp.float32)
            ok = (lower <= block) & (block < upper)
            top = jnp.max(s[j * D : (j + 1) * D], axis=0, keepdims=True)
            new = jnp.maximum(new, jnp.where(ok, top, LOW))
            allowed.append(ok)
        factor = jnp.exp2((m - new) * EXP2_SCALE)
        l = l * factor
        parts = []
        for j in range(BLOCKS):
            base = jnp.where(allowed[j], new * EXP2_SCALE, -LOW)
            p = jnp.exp2(s[j * D : (j + 1) * D] * EXP2_SCALE - base)
            l = l + jnp.sum(p.reshape(D // 8, 8, WIDE), axis=0)
            parts.append(p.astype(jnp.bfloat16))
        return jnp.concatenate(parts, axis=0), new, l, factor

    def collect(unit, p, acc, factor):
        c, _ = unit
        v = chunks[c][0:BLOCKS, 1].reshape(BLOCKS * D, D)
        return acc * factor + lax.dot_general(
            v, p, (((0,), (0,)), ((), ())), preferred_element_type=jnp.float32
        )

    ahead = score(units[0])
    pending = None
    for at, unit in enumerate(units):
        s = ahead
        if at + 1 < len(units):
            ahead = score(units[at + 1])
        w = unit[1]
        m, l, acc = state[w]
        p, m, l, factor = soften(unit, s, m, l)
        if pending is not None:
            u, p0, f0 = pending
            m0, l0, acc0 = state[u[1]]
            state[u[1]] = (m0, l0, collect(u, p0, acc0, f0))
        state[w] = (m, l, state[w][2])
        pending = (unit, p, factor)
    u, p0, f0 = pending
    m0, l0, acc0 = state[u[1]]
    state[u[1]] = (m0, l0, collect(u, p0, acc0, f0))

    for w in ws:
        m, l, acc = state[w]
        if half is not None:
            at = slice((w % per) * WIDE, (w % per + 1) * WIDE)
            out_ref[0:D, at] = acc
            out_ref[D : D + 8, at] = l
            out_ref[D + 8 : D + 16, at] = jnp.broadcast_to(m, (8, WIDE))
        else:
            m_out[:, cols[w]] = m
            l_out[:, cols[w]] = l
            acc_out[:, cols[w]] = acc


def attend(ids, packs, chunks, gain, state, half=None):
    first = state is None
    sums = (
        jax.ShapeDtypeStruct((1, 2 * ROWS), jnp.float32),
        jax.ShapeDtypeStruct((8, 2 * ROWS), jnp.float32),
        jax.ShapeDtypeStruct((D, 2 * ROWS), jnp.float32),
    )
    if half is not None:
        out_shape = jax.ShapeDtypeStruct((D + 16, ROWS), jnp.float32)
    elif first:
        out_shape = (jax.ShapeDtypeStruct((2 * ROWS, D), jnp.bfloat16),) + sums
    else:
        out_shape = sums
    extra = (gain,) if first else state
    n_keys = len(chunks) * BLOCKS * D
    rows = 2 * ROWS if half is None else ROWS

    def body(*refs):
        attention_kernel(len(chunks), first, half, *refs)

    out = pl.pallas_call(
        body,
        out_shape=out_shape,
        in_specs=[SMEM] + [VMEM] * (2 + len(chunks) + len(extra)),
        out_specs=VMEM if half is not None else (VMEM,) * len(out_shape),
        cost_estimate=pl.CostEstimate(
            flops=4 * rows * n_keys * D,
            bytes_accessed=n_keys * D * 4 + rows * D * 12,
            transcendentals=rows * n_keys,
        ),
        compiler_params=pltpu.CompilerParams(vmem_limit_bytes=16 << 20),
    )(ids, *packs, *chunks, *extra)
    if half is not None or first:
        return out
    return (state[0],) + tuple(out)


def merge_kernel(a_ref, b_ref, out_ref):
    a, b = a_ref[...], b_ref[...]
    top = jnp.maximum(a[D + 8 : D + 9], b[D + 8 : D + 9])
    fa = jnp.exp2((a[D + 8 : D + 9] - top) * EXP2_SCALE)
    fb = jnp.exp2((b[D + 8 : D + 9] - top) * EXP2_SCALE)
    total = jnp.sum(a[D : D + 8], axis=0, keepdims=True) * fa
    total = total + jnp.sum(b[D : D + 8], axis=0, keepdims=True) * fb
    o = (a[0:D] * fa + b[0:D] * fb) / total
    for h in range(HEADS):
        at = slice(h * TOK, (h + 1) * TOK)
        out_ref[:, at] = o[:, at].T.astype(jnp.bfloat16)


def merge(a, b):
    return pl.pallas_call(
        merge_kernel,
        out_shape=jax.ShapeDtypeStruct((TOK, ROWS), jnp.bfloat16),
        in_specs=[VMEM, VMEM],
        out_specs=VMEM,
        cost_estimate=pl.CostEstimate(
            flops=6 * ROWS * D, bytes_accessed=ROWS * D * 10, transcendentals=0
        ),
        compiler_params=pltpu.CompilerParams(vmem_limit_bytes=16 << 20),
    )(a, b)


def project_kernel(info_ref, *refs):
    slots, chunks, out_ref, held, done = refs[:4], refs[4:12], *refs[12:]
    rows = pl.ds(pl.multiple_of(info_ref[0] * 64, 64), 64)
    for p, chunk in enumerate(chunks):
        base = BLOCKS if p < 7 else 0
        for x in range(4):
            for y in range(2):
                tile = x * 2 + y
                pltpu.make_async_copy(
                    chunk.at[base + tile // 2, tile % 2, rows],
                    held.at[x, y * 8 + info_ref[2 + p]],
                    done,
                ).start()
    pltpu.make_async_copy(held, held, done).wait()
    total = None
    a = jnp.concatenate([slot[...] for slot in slots], axis=0)
    for x in range(4):
        w = jnp.concatenate(
            [held[x, :, t * 16 : (t + 1) * 16].reshape(256, 128) for t in range(4)],
            axis=1,
        )
        part = jnp.dot(
            a[:, x * 256 : (x + 1) * 256], w, preferred_element_type=jnp.float32
        )
        total = part if total is None else total + part
    for k in range(4):
        out_ref[(info_ref[1] + k) % 4] = total[k * TOK : (k + 1) * TOK]


def project(info, slots, chunks):
    return pl.pallas_call(
        project_kernel,
        out_shape=jax.ShapeDtypeStruct((4, TOK, 512), jnp.float32),
        in_specs=[SMEM] + [VMEM] * 4 + [pl.BlockSpec(memory_space=pl.ANY)] * 8,
        out_specs=VMEM,
        scratch_shapes=[
            pltpu.VMEM((4, 16, 64, 128), jnp.bfloat16),
            pltpu.SemaphoreType.DMA,
        ],
        cost_estimate=pl.CostEstimate(
            flops=512 * 1024 * 1024, bytes_accessed=3 << 20, transcendentals=0
        ),
        compiler_params=pltpu.CompilerParams(vmem_limit_bytes=16 << 20),
    )(info, *slots, *chunks)


def work(queries, keys, values, q_gain, frame_bounds, output_weight, attn_gate):
    ax, ay, az = lax.axis_index("x"), lax.axis_index("yh"), lax.axis_index("z")
    core = lax.axis_index("c")

    def trade(value, di=0, dy=0):
        pairs = []
        for i in range(2):
            for y in range(2):
                for a in range(2):
                    for c in range(2):
                        source = ((2 * i + a) * 2 + y) * 2 + c
                        x = 2 * ((i + di) % 2) + c
                        pairs.append((source, (x * 2 + (y + dy) % 2) * 2 + a))
        return lax.ppermute(value, ("x", "yh", "c"), pairs)

    quarter = output_weight[0].reshape(16, 4, 1, 8, 128).transpose(1, 2, 3, 0, 4)
    quarter = jnp.broadcast_to(quarter, (4, 2, 8, 16, 128)).reshape(1024, 128)
    quarter = lax.all_to_all(
        quarter, ("x", "yh"), split_axis=0, concat_axis=0, tiled=True
    )
    own = jnp.stack([keys, values])[None]
    chunk = jnp.concatenate(
        [
            trade(own),
            trade(own, di=1),
            trade(own, dy=1),
            trade(own, di=1, dy=1),
            quarter.reshape(4, 2, 128, 128),
        ]
    )
    block_x = 2 * (ax // 2) + core
    in_chunk = jnp.stack(
        [
            ((block_x + 2 * di) % 4) * 16 + ((ay + dy) % 2) * 8
            for dy in (0, 1)
            for di in (0, 1)
        ]
    ).astype(jnp.int32)
    hops = [0, -1, 1, -2, 2, -3, 3, -4]
    ids = [in_chunk + (az + h) % 8 for h in hops]

    bounds = jnp.pad(frame_bounds.astype(jnp.bfloat16), ((0, 14), (0, ROWS - TOK)))
    near = trade(jnp.concatenate([queries, bounds]))
    far = shift(near, "c", 1)
    packs = (near, far)

    right, left = [chunk], [chunk]
    for _ in range(1, 4):
        right.append(shift(right[-1], "z", 1))
        left.append(shift(left[-1], "z", -1))
    right.append(shift(right[3][:BLOCKS], "z", 1))
    left.append(shift(left[3][BLOCKS:], "z", -1))
    gain = q_gain[None, :]
    state = attend(ids[0], packs, [chunk], gain, None)
    for s in range(1, 4):
        state = attend(
            jnp.concatenate(ids[2 * s - 1 : 2 * s + 1]),
            packs,
            [right[s], left[s]],
            gain,
            state,
        )
    send = attend(ids[7], packs, [right[4]], gain, state, half=1)
    received = shift(send, "c", 1)
    keep = attend(ids[7], packs, [right[4]], gain, state, half=0)
    attended = merge(keep, received)

    slots = []
    for k in range(4):
        pairs = [
            (x * 2 + c, ((x + k + c) % 4) * 2 + x % 2) for x in range(4) for c in range(2)
        ]
        slots.append(lax.ppermute(attended, ("x", "c"), pairs))
    parts = [chunk, right[1], left[1], right[2], left[2], right[3], left[3]]
    parts.append(left[4])
    turn = (core + 4 - lax.axis_index("yl")) % 4
    info = [turn] + [(az + h) % 8 for h in hops]
    for_other = project(jnp.stack([1 - core] + info).astype(jnp.int32), slots, parts)
    from_other = shift(for_other, "c", 1)
    for_own = project(jnp.stack([core] + info).astype(jnp.int32), slots, parts)
    combined = for_own[0] + from_other[0]
    for s in range(1, 4):
        part = (for_own[s] + from_other[s]).astype(jnp.bfloat16)
        combined = combined + shift(part, "yl", s).astype(jnp.float32)
    result = (jnp.tanh(attn_gate[0]) * combined).astype(jnp.bfloat16)
    pairs = [(x * 4 + y, ((x - y) % 4) * 4 + x) for x in range(4) for y in range(4)]
    return lax.ppermute(result, ("x", "yl"), pairs)


def solution(mesh):
    fine = Mesh(mesh.devices.reshape(4, 2, 8, 4, 2), ("x", "yh", "z", "yl", "c"))
    group = ("yl", "c")
    placed = (
        P(FRAMES, group),
        P(FRAMES, group),
        P(FRAMES, group),
        P(),
        P(None, FRAMES),
        P(group, FRAMES, None),
        P(),
    )
    return jax.shard_map(
        work, mesh=fine, in_specs=placed, out_specs=P(FRAMES, group), check_vma=False
    )
```

```python
import math

import jax
import jax.numpy as jnp
from jax import lax
from jax.experimental import pallas as pl
from jax.experimental.pallas import tpu as pltpu
from jax.sharding import Mesh, PartitionSpec as P


D = 128
HEADS = 8
TOK = 128
ROWS = HEADS * TOK
BLOCKS = 4
WIDE = 256
PACK = TOK + 16
LOW = -1e30
EXP2_SCALE = math.log2(math.e) / math.sqrt(D)
VMEM = pl.BlockSpec(memory_space=pltpu.VMEM)
SMEM = pl.BlockSpec(memory_space=pltpu.SMEM)
FRAMES = ("x", "yh", "z")


def shift(value, axis, steps):
    count = lax.axis_size(axis)
    return lax.ppermute(value, axis, [(s, (s + steps) % count) for s in range(count)])


def attention_kernel(offset, n_chunks, first, half, ids_ref, *refs):
    refs = list(refs)
    packs = [refs.pop(0) for _ in range(2)]
    chunks = [refs.pop(0) for _ in range(n_chunks)]
    if first:
        gain_ref = refs.pop(0)
    else:
        nq_ref, m_in, l_in, acc_in = [refs.pop(0) for _ in range(4)]
    if half is not None:
        out_ref = refs.pop(0)
    elif first:
        nq_ref, m_out, l_out, acc_out = [refs.pop(0) for _ in range(4)]
    else:
        m_out, l_out, acc_out = [refs.pop(0) for _ in range(3)]
    if first:
        for b, pack in enumerate(packs):
            for h in range(HEADS):
                x = pack[0:TOK, h * D : (h + 1) * D].astype(jnp.float32)
                mean = jnp.mean(x * x, axis=-1, keepdims=True)
                x = x * lax.rsqrt(mean + 1e-05) * gain_ref[...]
                at = b * ROWS + h * TOK
                nq_ref[at : at + TOK, :] = x.astype(jnp.bfloat16)
    limits = []
    for pack in packs:
        rows = pack[TOK:PACK, 0:TOK].astype(jnp.float32)
        rows = jnp.concatenate([rows] * (WIDE // TOK), axis=1)
        limits.append((rows[0:1], rows[1:2]))
    per = ROWS // WIDE
    ws = range(2 * per) if half is None else range(half * per, (half + 1) * per)
    cols = {w: slice(w * WIDE, (w + 1) * WIDE) for w in ws}
    if first:
        state = {
            w: (
                jnp.full((1, WIDE), LOW, jnp.float32),
                jnp.zeros((8, WIDE), jnp.float32),
                jnp.zeros((D, WIDE), jnp.float32),
            )
            for w in ws
        }
    else:
        state = {w: (m_in[:, cols[w]], l_in[:, cols[w]], acc_in[:, cols[w]]) for w in ws}
    units = [(c, w) for c in range(n_chunks) for w in ws]

    def score(unit):
        c, w = unit
        k = chunks[c][0:BLOCKS, 0].reshape(BLOCKS * D, D)
        return lax.dot_general(
            k,
            nq_ref[cols[w], :],
            (((1,), (1,)), ((), ())),
            preferred_element_type=jnp.float32,
        )

    def soften(unit, s, m, l):
        c, w = unit
        lower, upper = limits[w // per]
        allowed = []
        new = m
        for j in range(BLOCKS):
            block = ids_ref[(offset + c) * BLOCKS + j].astype(jnp.float32)
            ok = (lower <= block) & (block < upper)
            top = jnp.max(s[j * D : (j + 1) * D], axis=0, keepdims=True)
            new = jnp.maximum(new, jnp.where(ok, top, LOW))
            allowed.append(ok)
        factor = jnp.exp2((m - new) * EXP2_SCALE)
        l = l * factor
        parts = []
        for j in range(BLOCKS):
            base = jnp.where(allowed[j], new * EXP2_SCALE, -LOW)
            p = jnp.exp2(s[j * D : (j + 1) * D] * EXP2_SCALE - base)
            l = l + jnp.sum(p.reshape(D // 8, 8, WIDE), axis=0)
            parts.append(p.astype(jnp.bfloat16))
        return jnp.concatenate(parts, axis=0), new, l, factor

    def collect(unit, p, acc, factor):
        c, _ = unit
        v = chunks[c][0:BLOCKS, 1].reshape(BLOCKS * D, D)
        return acc * factor + lax.dot_general(
            v, p, (((0,), (0,)), ((), ())), preferred_element_type=jnp.float32
        )

    ahead = score(units[0])
    pending = None
    for at, unit in enumerate(units):
        s = ahead
        if at + 1 < len(units):
            ahead = score(units[at + 1])
        w = unit[1]
        m, l, acc = state[w]
        p, m, l, factor = soften(unit, s, m, l)
        if pending is not None:
            u, p0, f0 = pending
            m0, l0, acc0 = state[u[1]]
            state[u[1]] = (m0, l0, collect(u, p0, acc0, f0))
        state[w] = (m, l, state[w][2])
        pending = (unit, p, factor)
    u, p0, f0 = pending
    m0, l0, acc0 = state[u[1]]
    state[u[1]] = (m0, l0, collect(u, p0, acc0, f0))

    for w in ws:
        m, l, acc = state[w]
        if half is not None:
            at = slice((w % per) * WIDE, (w % per + 1) * WIDE)
            out_ref[0:D, at] = acc
            out_ref[D : D + 8, at] = l
            out_ref[D + 8 : D + 16, at] = jnp.broadcast_to(m, (8, WIDE))
        else:
            m_out[:, cols[w]] = m
            l_out[:, cols[w]] = l
            acc_out[:, cols[w]] = acc


def attend(ids, offset, packs, chunks, gain, state, half=None):
    first = state is None
    sums = (
        jax.ShapeDtypeStruct((1, 2 * ROWS), jnp.float32),
        jax.ShapeDtypeStruct((8, 2 * ROWS), jnp.float32),
        jax.ShapeDtypeStruct((D, 2 * ROWS), jnp.float32),
    )
    if half is not None:
        out_shape = jax.ShapeDtypeStruct((D + 16, ROWS), jnp.float32)
    elif first:
        out_shape = (jax.ShapeDtypeStruct((2 * ROWS, D), jnp.bfloat16),) + sums
    else:
        out_shape = sums
    extra = (gain,) if first else state
    n_keys = len(chunks) * BLOCKS * D
    rows = 2 * ROWS if half is None else ROWS

    def body(*refs):
        attention_kernel(offset, len(chunks), first, half, *refs)

    out = pl.pallas_call(
        body,
        out_shape=out_shape,
        in_specs=[SMEM] + [VMEM] * (2 + len(chunks) + len(extra)),
        out_specs=VMEM if half is not None else (VMEM,) * len(out_shape),
        cost_estimate=pl.CostEstimate(
            flops=4 * rows * n_keys * D,
            bytes_accessed=n_keys * D * 4 + rows * D * 12,
            transcendentals=rows * n_keys,
        ),
        compiler_params=pltpu.CompilerParams(vmem_limit_bytes=16 << 20),
    )(ids, *packs, *chunks, *extra)
    if half is not None or first:
        return out
    return (state[0],) + tuple(out)


def merge_kernel(a_ref, b_ref, out_ref):
    a, b = a_ref[...], b_ref[...]
    top = jnp.maximum(a[D + 8 : D + 9], b[D + 8 : D + 9])
    fa = jnp.exp2((a[D + 8 : D + 9] - top) * EXP2_SCALE)
    fb = jnp.exp2((b[D + 8 : D + 9] - top) * EXP2_SCALE)
    total = jnp.sum(a[D : D + 8], axis=0, keepdims=True) * fa
    total = total + jnp.sum(b[D : D + 8], axis=0, keepdims=True) * fb
    o = (a[0:D] * fa + b[0:D] * fb) / total
    for h in range(HEADS):
        at = slice(h * TOK, (h + 1) * TOK)
        out_ref[:, at] = o[:, at].T.astype(jnp.bfloat16)


def merge(a, b):
    return pl.pallas_call(
        merge_kernel,
        out_shape=jax.ShapeDtypeStruct((TOK, ROWS), jnp.bfloat16),
        in_specs=[VMEM, VMEM],
        out_specs=VMEM,
        cost_estimate=pl.CostEstimate(
            flops=6 * ROWS * D, bytes_accessed=ROWS * D * 10, transcendentals=0
        ),
        compiler_params=pltpu.CompilerParams(vmem_limit_bytes=16 << 20),
    )(a, b)


def assemble_kernel(at_ref, *refs):
    chunks, out_ref = refs[:8], refs[8]
    for p in range(8):
        for y in range(2):
            for x in range(4):
                tile = x * 2 + y
                block = chunks[p][BLOCKS + tile // 2, tile % 2]
                for t in range(8):
                    out_ref[x, y * 8 + at_ref[p], :, t * 128 : (t + 1) * 128] = block[
                        t * 16 : (t + 1) * 16
                    ]


def assemble(at, chunks):
    return pl.pallas_call(
        assemble_kernel,
        out_shape=jax.ShapeDtypeStruct((4, 16, 16, 1024), jnp.bfloat16),
        in_specs=[SMEM] + [VMEM] * 8,
        out_specs=VMEM,
        cost_estimate=pl.CostEstimate(
            flops=0, bytes_accessed=4 << 20, transcendentals=0
        ),
        compiler_params=pltpu.CompilerParams(vmem_limit_bytes=16 << 20),
    )(at, *chunks)


def project_kernel(col_ref, turn_ref, a0, a1, a2, a3, w_ref, out_ref):
    total = None
    a = jnp.concatenate([a0[...], a1[...], a2[...], a3[...]], axis=0)
    for x in range(4):
        part = jnp.dot(
            a[:, x * 256 : (x + 1) * 256],
            w_ref[x].reshape(256, 512),
            preferred_element_type=jnp.float32,
        )
        total = part if total is None else total + part
    for k in range(4):
        out_ref[(turn_ref[0] + k) % 4] = total[k * TOK : (k + 1) * TOK]


def project(column, turn, slots, weight):
    return pl.pallas_call(
        project_kernel,
        grid_spec=pltpu.PrefetchScalarGridSpec(
            num_scalar_prefetch=2,
            grid=(1,),
            in_specs=[pl.BlockSpec((TOK, ROWS), lambda i, col, turn: (0, 0))] * 4
            + [
                pl.BlockSpec((4, 16, 16, 512), lambda i, col, turn: (0, 0, 0, col[0])),
            ],
            out_specs=pl.BlockSpec((4, TOK, 512), lambda i, col, turn: (0, 0, 0)),
        ),
        out_shape=jax.ShapeDtypeStruct((4, TOK, 512), jnp.float32),
        cost_estimate=pl.CostEstimate(
            flops=512 * 1024 * 1024, bytes_accessed=3 << 20, transcendentals=0
        ),
        compiler_params=pltpu.CompilerParams(vmem_limit_bytes=16 << 20),
    )(column, turn, *slots, weight)


def work(queries, keys, values, q_gain, frame_bounds, output_weight, attn_gate):
    ax, ay, az = lax.axis_index("x"), lax.axis_index("yh"), lax.axis_index("z")
    core = lax.axis_index("c")

    def trade(value, di=0, dy=0):
        pairs = []
        for i in range(2):
            for y in range(2):
                for a in range(2):
                    for c in range(2):
                        source = ((2 * i + a) * 2 + y) * 2 + c
                        x = 2 * ((i + di) % 2) + c
                        pairs.append((source, (x * 2 + (y + dy) % 2) * 2 + a))
        return lax.ppermute(value, ("x", "yh", "c"), pairs)

    quarter = output_weight[0].reshape(16, 4, 1, 8, 128).transpose(1, 2, 3, 0, 4)
    quarter = jnp.broadcast_to(quarter, (4, 2, 8, 16, 128)).reshape(1024, 128)
    quarter = lax.all_to_all(
        quarter, ("x", "yh"), split_axis=0, concat_axis=0, tiled=True
    )
    own = jnp.stack([keys, values])[None]
    pair = jnp.concatenate([trade(own), trade(own, dy=1)])
    across = shift(pair, "x", 2)
    chunk = jnp.concatenate([pair, across, quarter.reshape(4, 2, 128, 128)])
    block_x = 2 * (ax // 2) + core
    in_chunk = jnp.stack(
        [
            ((block_x + 2 * di) % 4) * 16 + ((ay + dy) % 2) * 8
            for di in (0, 1)
            for dy in (0, 1)
        ]
    ).astype(jnp.int32)
    hops = [0, -1, 1, -2, 2, -3, 3, -4]
    at = (az + jnp.array(hops, jnp.int32)) % 8
    ids = (at[:, None] + in_chunk[None, :]).reshape(-1)

    bounds = jnp.pad(frame_bounds.astype(jnp.bfloat16), ((0, 14), (0, ROWS - TOK)))
    near = trade(jnp.concatenate([queries, bounds]))
    far = shift(near, "c", 1)
    packs = (near, far)

    right, left = [chunk], [chunk]
    for s in range(1, 5):
        right.append(shift(right[-1], "z", 1))
        if s < 4:
            left.append(shift(left[-1], "z", -1))
    gain = q_gain[None, :]
    state = attend(ids, 0, packs, [chunk], gain, None)
    for s in range(1, 4):
        state = attend(
            ids,
            2 * s - 1,
            packs,
            [right[s], left[s]],
            gain,
            state,
        )
    send = attend(ids, 7, packs, [right[4]], gain, state, half=1)
    received = shift(send, "c", 1)
    keep = attend(ids, 7, packs, [right[4]], gain, state, half=0)
    attended = merge(keep, received)

    slots = []
    for k in range(4):
        pairs = [
            (x * 2 + c, ((x + k + c) % 4) * 2 + x % 2) for x in range(4) for c in range(2)
        ]
        slots.append(lax.ppermute(attended, ("x", "c"), pairs))
    parts = [chunk, right[1], left[1], right[2], left[2], right[3], left[3], right[4]]
    weight = assemble(at, parts)

    core = core.astype(jnp.int32)[None]
    turn = (core + 4 - lax.axis_index("yl")) % 4
    for_other = project(1 - core, turn, slots, weight)
    from_other = shift(for_other, "c", 1)
    for_own = project(core, turn, slots, weight)
    combined = for_own[0] + from_other[0]
    for s in range(1, 4):
        part = (for_own[s] + from_other[s]).astype(jnp.bfloat16)
        combined = combined + shift(part, "yl", s).astype(jnp.float32)
    result = (jnp.tanh(attn_gate[0]) * combined).astype(jnp.bfloat16)
    pairs = [(x * 4 + y, ((x - y) % 4) * 4 + x) for x in range(4) for y in range(4)]
    return lax.ppermute(result, ("x", "yl"), pairs)


def solution(mesh):
    fine = Mesh(mesh.devices.reshape(4, 2, 8, 4, 2), ("x", "yh", "z", "yl", "c"))
    group = ("yl", "c")
    placed = (
        P(FRAMES, group),
        P(FRAMES, group),
        P(FRAMES, group),
        P(),
        P(None, FRAMES),
        P(group, FRAMES, None),
        P(),
    )
    return jax.shard_map(
        work, mesh=fine, in_specs=placed, out_specs=P(FRAMES, group), check_vma=False
    )
```

```python
import math

import jax
import jax.numpy as jnp
from jax import lax
from jax.experimental import pallas as pl
from jax.experimental.pallas import tpu as pltpu
from jax.sharding import Mesh, PartitionSpec as P


D = 128
HEADS = 8
TOK = 128
ROWS = HEADS * TOK
BLOCKS = 4
WIDE = 256
PACK = TOK + 16
LOW = -1e30
EXP2_SCALE = math.log2(math.e) / math.sqrt(D)
VMEM = pl.BlockSpec(memory_space=pltpu.VMEM)
SMEM = pl.BlockSpec(memory_space=pltpu.SMEM)
FRAMES = ("x", "yh", "z")


def shift(value, axis, steps):
    count = lax.axis_size(axis)
    return lax.ppermute(value, axis, [(s, (s + steps) % count) for s in range(count)])


def attention_kernel(offset, n_chunks, first, half, ids_ref, *refs):
    refs = list(refs)
    packs = [refs.pop(0) for _ in range(2)]
    chunks = [refs.pop(0) for _ in range(n_chunks)]
    if first:
        gain_ref = refs.pop(0)
    else:
        nq_ref, m_in, l_in, acc_in = [refs.pop(0) for _ in range(4)]
    if half is not None:
        out_ref = refs.pop(0)
    elif first:
        nq_ref, m_out, l_out, acc_out = [refs.pop(0) for _ in range(4)]
    else:
        m_out, l_out, acc_out = [refs.pop(0) for _ in range(3)]
    if first:
        for b, pack in enumerate(packs):
            for h in range(HEADS):
                x = pack[0:TOK, h * D : (h + 1) * D].astype(jnp.float32)
                mean = jnp.mean(x * x, axis=-1, keepdims=True)
                x = x * lax.rsqrt(mean + 1e-05) * gain_ref[...]
                at = b * ROWS + h * TOK
                nq_ref[at : at + TOK, :] = x.astype(jnp.bfloat16)
    limits = []
    for pack in packs:
        rows = pack[TOK:PACK, 0:TOK].astype(jnp.float32)
        rows = jnp.concatenate([rows] * (WIDE // TOK), axis=1)
        limits.append((rows[0:1], rows[1:2]))
    per = ROWS // WIDE
    ws = range(2 * per) if half is None else range(half * per, (half + 1) * per)
    cols = {w: slice(w * WIDE, (w + 1) * WIDE) for w in ws}
    if first:
        state = {
            w: (
                jnp.full((1, WIDE), LOW, jnp.float32),
                jnp.zeros((8, WIDE), jnp.float32),
                jnp.zeros((D, WIDE), jnp.float32),
            )
            for w in ws
        }
    else:
        state = {w: (m_in[:, cols[w]], l_in[:, cols[w]], acc_in[:, cols[w]]) for w in ws}
    units = [(c, w) for c in range(n_chunks) for w in ws]

    def score(unit):
        c, w = unit
        k = chunks[c][0:BLOCKS, 0].reshape(BLOCKS * D, D)
        return lax.dot_general(
            k,
            nq_ref[cols[w], :],
            (((1,), (1,)), ((), ())),
            preferred_element_type=jnp.float32,
        )

    def soften(unit, s, m, l):
        c, w = unit
        lower, upper = limits[w // per]
        allowed = []
        new = m
        for j in range(BLOCKS):
            block = ids_ref[(offset + c) * BLOCKS + j].astype(jnp.float32)
            ok = (lower <= block) & (block < upper)
            top = jnp.max(s[j * D : (j + 1) * D], axis=0, keepdims=True)
            new = jnp.maximum(new, jnp.where(ok, top, LOW))
            allowed.append(ok)
        factor = jnp.exp2((m - new) * EXP2_SCALE)
        l = l * factor
        parts = []
        for j in range(BLOCKS):
            base = jnp.where(allowed[j], new * EXP2_SCALE, -LOW)
            p = jnp.exp2(s[j * D : (j + 1) * D] * EXP2_SCALE - base)
            l = l + jnp.sum(p.reshape(D // 8, 8, WIDE), axis=0)
            parts.append(p.astype(jnp.bfloat16))
        return jnp.concatenate(parts, axis=0), new, l, factor

    def collect(unit, p, acc, factor):
        c, _ = unit
        v = chunks[c][0:BLOCKS, 1].reshape(BLOCKS * D, D)
        return acc * factor + lax.dot_general(
            v, p, (((0,), (0,)), ((), ())), preferred_element_type=jnp.float32
        )

    ahead = score(units[0])
    pending = None
    for at, unit in enumerate(units):
        s = ahead
        if at + 1 < len(units):
            ahead = score(units[at + 1])
        w = unit[1]
        m, l, acc = state[w]
        p, m, l, factor = soften(unit, s, m, l)
        if pending is not None:
            u, p0, f0 = pending
            m0, l0, acc0 = state[u[1]]
            state[u[1]] = (m0, l0, collect(u, p0, acc0, f0))
        state[w] = (m, l, state[w][2])
        pending = (unit, p, factor)
    u, p0, f0 = pending
    m0, l0, acc0 = state[u[1]]
    state[u[1]] = (m0, l0, collect(u, p0, acc0, f0))

    for w in ws:
        m, l, acc = state[w]
        if half is not None:
            at = slice((w % per) * WIDE, (w % per + 1) * WIDE)
            out_ref[0:D, at] = acc
            out_ref[D : D + 8, at] = l
            out_ref[D + 8 : D + 16, at] = jnp.broadcast_to(m, (8, WIDE))
        else:
            m_out[:, cols[w]] = m
            l_out[:, cols[w]] = l
            acc_out[:, cols[w]] = acc


def attend(ids, offset, packs, chunks, gain, state, half=None):
    first = state is None
    sums = (
        jax.ShapeDtypeStruct((1, 2 * ROWS), jnp.float32),
        jax.ShapeDtypeStruct((8, 2 * ROWS), jnp.float32),
        jax.ShapeDtypeStruct((D, 2 * ROWS), jnp.float32),
    )
    if half is not None:
        out_shape = jax.ShapeDtypeStruct((D + 16, ROWS), jnp.float32)
    elif first:
        out_shape = (jax.ShapeDtypeStruct((2 * ROWS, D), jnp.bfloat16),) + sums
    else:
        out_shape = sums
    extra = (gain,) if first else state
    n_keys = len(chunks) * BLOCKS * D
    rows = 2 * ROWS if half is None else ROWS

    def body(*refs):
        attention_kernel(offset, len(chunks), first, half, *refs)

    out = pl.pallas_call(
        body,
        out_shape=out_shape,
        in_specs=[SMEM] + [VMEM] * (2 + len(chunks) + len(extra)),
        out_specs=VMEM if half is not None else (VMEM,) * len(out_shape),
        cost_estimate=pl.CostEstimate(
            flops=4 * rows * n_keys * D,
            bytes_accessed=n_keys * D * 4 + rows * D * 12,
            transcendentals=rows * n_keys,
        ),
        compiler_params=pltpu.CompilerParams(vmem_limit_bytes=16 << 20),
    )(ids, *packs, *chunks, *extra)
    if half is not None or first:
        return out
    return (state[0],) + tuple(out)


def merge_kernel(a_ref, b_ref, out_ref):
    a, b = a_ref[...], b_ref[...]
    top = jnp.maximum(a[D + 8 : D + 9], b[D + 8 : D + 9])
    fa = jnp.exp2((a[D + 8 : D + 9] - top) * EXP2_SCALE)
    fb = jnp.exp2((b[D + 8 : D + 9] - top) * EXP2_SCALE)
    total = jnp.sum(a[D : D + 8], axis=0, keepdims=True) * fa
    total = total + jnp.sum(b[D : D + 8], axis=0, keepdims=True) * fb
    o = (a[0:D] * fa + b[0:D] * fb) / total
    for h in range(HEADS):
        at = slice(h * TOK, (h + 1) * TOK)
        out_ref[:, at] = o[:, at].T.astype(jnp.bfloat16)


def merge(a, b):
    return pl.pallas_call(
        merge_kernel,
        out_shape=jax.ShapeDtypeStruct((TOK, ROWS), jnp.bfloat16),
        in_specs=[VMEM, VMEM],
        out_specs=VMEM,
        cost_estimate=pl.CostEstimate(
            flops=6 * ROWS * D, bytes_accessed=ROWS * D * 10, transcendentals=0
        ),
        compiler_params=pltpu.CompilerParams(vmem_limit_bytes=16 << 20),
    )(a, b)


def assemble_kernel(at_ref, *refs):
    chunks, out_ref = refs[:8], refs[8]
    for p in range(8):
        for y in range(2):
            for x in range(4):
                tile = x * 2 + y
                block = chunks[p][tile // 2, tile % 2]
                for t in range(8):
                    out_ref[x, y * 8 + at_ref[p], :, t * 128 : (t + 1) * 128] = block[
                        t * 16 : (t + 1) * 16
                    ]


def assemble(at, chunks):
    return pl.pallas_call(
        assemble_kernel,
        out_shape=jax.ShapeDtypeStruct((4, 16, 16, 1024), jnp.bfloat16),
        in_specs=[SMEM] + [VMEM] * 8,
        out_specs=VMEM,
        cost_estimate=pl.CostEstimate(
            flops=0, bytes_accessed=4 << 20, transcendentals=0
        ),
        compiler_params=pltpu.CompilerParams(vmem_limit_bytes=16 << 20),
    )(at, *chunks)


def project_kernel(col_ref, turn_ref, a0, a1, a2, a3, w_ref, out_ref):
    total = None
    a = jnp.concatenate([a0[...], a1[...], a2[...], a3[...]], axis=0)
    for x in range(4):
        part = jnp.dot(
            a[:, x * 256 : (x + 1) * 256],
            w_ref[x].reshape(256, 512),
            preferred_element_type=jnp.float32,
        )
        total = part if total is None else total + part
    for k in range(4):
        out_ref[(turn_ref[0] + k) % 4] = total[k * TOK : (k + 1) * TOK]


def project(column, turn, slots, weight):
    return pl.pallas_call(
        project_kernel,
        grid_spec=pltpu.PrefetchScalarGridSpec(
            num_scalar_prefetch=2,
            grid=(1,),
            in_specs=[pl.BlockSpec((TOK, ROWS), lambda i, col, turn: (0, 0))] * 4
            + [
                pl.BlockSpec((4, 16, 16, 512), lambda i, col, turn: (0, 0, 0, col[0])),
            ],
            out_specs=pl.BlockSpec((4, TOK, 512), lambda i, col, turn: (0, 0, 0)),
        ),
        out_shape=jax.ShapeDtypeStruct((4, TOK, 512), jnp.float32),
        cost_estimate=pl.CostEstimate(
            flops=512 * 1024 * 1024, bytes_accessed=3 << 20, transcendentals=0
        ),
        compiler_params=pltpu.CompilerParams(vmem_limit_bytes=16 << 20),
    )(column, turn, *slots, weight)


def work(queries, keys, values, q_gain, frame_bounds, output_weight, attn_gate):
    ax, ay, az = lax.axis_index("x"), lax.axis_index("yh"), lax.axis_index("z")
    core = lax.axis_index("c")

    def trade(value, di=0, dy=0):
        pairs = []
        for i in range(2):
            for y in range(2):
                for a in range(2):
                    for c in range(2):
                        source = ((2 * i + a) * 2 + y) * 2 + c
                        x = 2 * ((i + di) % 2) + c
                        pairs.append((source, (x * 2 + (y + dy) % 2) * 2 + a))
        return lax.ppermute(value, ("x", "yh", "c"), pairs)

    quarter = output_weight[0].reshape(16, 4, 1, 8, 128).transpose(1, 2, 3, 0, 4)
    quarter = jnp.broadcast_to(quarter, (4, 2, 8, 16, 128)).reshape(1024, 128)
    quarter = lax.all_to_all(
        quarter, ("x", "yh"), split_axis=0, concat_axis=0, tiled=True
    )
    own = jnp.stack([keys, values])[None]
    pair = jnp.concatenate([trade(own), trade(own, dy=1)])
    across = shift(pair, "x", 2)
    chunk = jnp.concatenate([pair, across, quarter.reshape(4, 2, 128, 128)])
    block_x = 2 * (ax // 2) + core
    in_chunk = jnp.stack(
        [
            ((block_x + 2 * di) % 4) * 16 + ((ay + dy) % 2) * 8
            for di in (0, 1)
            for dy in (0, 1)
        ]
    ).astype(jnp.int32)
    hops = [0, -1, 1, -2, 2, -3, 3, -4]
    at = (az + jnp.array(hops, jnp.int32)) % 8
    ids = (at[:, None] + in_chunk[None, :]).reshape(-1)

    bounds = jnp.pad(frame_bounds.astype(jnp.bfloat16), ((0, 14), (0, ROWS - TOK)))
    near = trade(jnp.concatenate([queries, bounds]))
    far = shift(near, "c", 1)
    packs = (near, far)

    right, left = [chunk], [chunk]
    for _ in range(1, 4):
        right.append(shift(right[-1], "z", 1))
        left.append(shift(left[-1], "z", -1))
    right.append(shift(right[3][:BLOCKS], "z", 1))
    left.append(shift(left[3][BLOCKS:], "z", -1))
    gain = q_gain[None, :]
    state = attend(ids, 0, packs, [chunk], gain, None)
    for s in range(1, 4):
        state = attend(
            ids,
            2 * s - 1,
            packs,
            [right[s], left[s]],
            gain,
            state,
        )
    send = attend(ids, 7, packs, [right[4]], gain, state, half=1)
    received = shift(send, "c", 1)
    keep = attend(ids, 7, packs, [right[4]], gain, state, half=0)
    attended = merge(keep, received)

    slots = []
    for k in range(4):
        pairs = [
            (x * 2 + c, ((x + k + c) % 4) * 2 + x % 2) for x in range(4) for c in range(2)
        ]
        slots.append(lax.ppermute(attended, ("x", "c"), pairs))
    parts = []
    for s in range(4):
        parts += [c[BLOCKS:] for c in ([chunk] if s == 0 else [right[s], left[s]])]
    parts.append(left[4])
    weight = assemble(at, parts)

    core = core.astype(jnp.int32)[None]
    turn = (core + 4 - lax.axis_index("yl")) % 4
    for_other = project(1 - core, turn, slots, weight)
    from_other = shift(for_other, "c", 1)
    for_own = project(core, turn, slots, weight)
    combined = for_own[0] + from_other[0]
    for s in range(1, 4):
        part = (for_own[s] + from_other[s]).astype(jnp.bfloat16)
        combined = combined + shift(part, "yl", s).astype(jnp.float32)
    result = (jnp.tanh(attn_gate[0]) * combined).astype(jnp.bfloat16)
    pairs = [(x * 4 + y, ((x - y) % 4) * 4 + x) for x in range(4) for y in range(4)]
    return lax.ppermute(result, ("x", "yl"), pairs)


def solution(mesh):
    fine = Mesh(mesh.devices.reshape(4, 2, 8, 4, 2), ("x", "yh", "z", "yl", "c"))
    group = ("yl", "c")
    placed = (
        P(FRAMES, group),
        P(FRAMES, group),
        P(FRAMES, group),
        P(),
        P(None, FRAMES),
        P(group, FRAMES, None),
        P(),
    )
    return jax.shard_map(
        work, mesh=fine, in_specs=placed, out_specs=P(FRAMES, group), check_vma=False
    )
```
